32 devices in a mesh: groups: 2 (over y), hist: 4 (over z), tower: 2 (over x), head: 2 (over core).
Axes of the slice: x: 2, y: 2, z: 4, core: 2. Of those that a mesh axis runs over, the one named last changes fastest.
Arguments:
- queries: bfloat16 [1024, 1024], P(('groups', 'hist', 'tower'), 'head'), parts along dimension 0, may hold values from -6 to 6
- hist_keys: bfloat16 [4, 1024, 1024], P('groups', 'hist', 'head'), parts along dimension 0, may hold values from -6 to 6
- hist_values: bfloat16 [4, 1024, 1024], P('groups', 'hist', 'head'), parts along dimension 0, may hold values from -6 to 6
- cand_user: int32 [1024], P(('groups', 'hist', 'tower')), parts along dimension 0, may hold values from 0 to 1
- time_bucket: int32 [4, 1024], P('groups', 'hist'), parts along dimension 0, may hold values from 0 to 127
- hist_len: int32 [4], P('groups'), parts along dimension 0, may hold values from 256 to 1024
- cand_gate: bfloat16 [1024, 1024], P(('groups', 'hist', 'tower'), 'head'), parts along dimension 0, may hold values from -6 to 6
- time_bias: float32 [128, 8], P(None, 'head'), may hold values from -4 to 4
- tower_in: bfloat16 [1024, 4096], P('head', 'tower'), may hold values from -0.1875 to 0.1875
- tower_bias: float32 [4096], P('tower'), may hold values from -4 to 4
- tower_out: float32 [4096], P('tower'), may hold values from -0.09375 to 0.09375
Outputs:
- cand_states: bfloat16 [1024, 1024], P(('groups', 'hist', 'tower'), 'head'), parts along dimension 0
- cand_scores: float32 [1024], P(('groups', 'hist', 'tower')), parts along dimension 0
The draws below stay inside these ranges and needn't reach their ends.
There are 2 independent parts, one for each index of `groups`. The reference program is written for one: setup_inputs(seed, part) draws one part's arguments, and reference() takes and returns one part's arrays. A program takes and returns all parts, laid end to end along the dimension named above; an argument that names none is the same for every part. Nothing has to cross between parts.
All inputs are finite; a program needn't handle non-finite values.
Results may differ from the reference program's by a relative error of at most 0.017.
Values may be sent and summed in bfloat16 or wider, within the bound.
A program may use at most 64 MiB of HBM per device.

```python
import jax
import jax.numpy as jnp
from jax import lax

D = 1024
H = 8
DH = 128
FF = 4096
NB = 128
USERS = 2
HL_DEV = 256
HLEN = 1024
CANDS = 512
N_HIST = 4


def set_ends(entries, stream_key, low, largest):
    longest = entries.shape.index(max(entries.shape))
    spots = []
    for shift in (0, 1):
        where = [jax.random.randint(jax.random.fold_in(stream_key, axis), (), 0, length) for axis, length in enumerate(entries.shape)]
        where[longest] = (where[longest] + shift) % entries.shape[longest]
        spots.append(tuple(where))
    return entries.at[spots[0]].set(low).at[spots[1]].set(largest)


def steps_of(rng, dims, pieces, least, top_value):
    level, own = 1.0, jax.random.fold_in(rng, 6)
    for position, shards_of in pieces:
        steps = jnp.exp(jax.random.uniform(jax.random.fold_in(own, position), (shards_of,), jnp.float32, least / len(pieces), top_value / len(pieces)))
        level = level * jnp.repeat(steps, dims[position] // shards_of).reshape([-1 if axis == position else 1 for axis in range(len(dims))])
    return level


def centred(own_key, shape, scale, reach, pieces=(), kind=jnp.bfloat16):
    drawn = jax.random.normal(own_key, shape, jnp.float32) * scale
    if len(pieces) > 0:
        drawn = steps_of(own_key, shape, pieces, -0.22, 0.18) * drawn
    return jnp.clip(drawn, min=-reach, max=reach).astype(kind)


def setup_inputs(seed: int = 0, part: int = 0) -> dict:
    keys = jax.random.split(jax.random.key(seed), 12)
    part_splits = jax.random.split(jax.random.fold_in(keys[11], part), 12)
    return {
        "queries": centred(part_splits[0], (CANDS, D), 1.0, 6.0, ((0, 8), (1, 2))),
        "hist_keys": centred(part_splits[1], (USERS, HLEN, D), 1.0, 6.0, ((1, 4), (2, 2))),
        "hist_values": centred(part_splits[2], (USERS, HLEN, D), 1.0, 6.0, ((1, 4), (2, 2))),
        "cand_user": set_ends(jax.random.randint(part_splits[3], (CANDS,), 0, USERS), jax.random.fold_in(part_splits[3], 1), 0, USERS - 1).astype(jnp.int32),
        "time_bucket": set_ends(jax.random.randint(part_splits[4], (USERS, HLEN), 0, NB), jax.random.fold_in(part_splits[4], 1), 0, NB - 1).astype(jnp.int32),
        "hist_len": jax.random.randint(part_splits[5], (USERS,), HLEN // 4, HLEN + 1).astype(jnp.int32),
        "cand_gate": centred(part_splits[6], (CANDS, D), 1.0, 6.0, ((0, 8), (1, 2))),
        "time_bias": centred(keys[7], (NB, H), 1.0, 4.0, ((1, 2),), jnp.float32),
        "tower_in": centred(keys[8], (D, FF), D ** -0.5, 0.1875, ((0, 2), (1, 2))),
        "tower_bias": centred(keys[9], (FF,), 1.0, 4.0, ((0, 2),), jnp.float32),
        "tower_out": centred(keys[10], (FF,), FF ** -0.5, 0.09375, ((0, 2),), jnp.float32),
    }


def reference(queries, hist_keys, hist_values, cand_user, time_bucket, hist_len, cand_gate, time_bias, tower_in, tower_bias, tower_out):
    score_scale = DH ** (-0.5)
    positions = jnp.arange(HLEN, dtype=jnp.int32)
    key_live = positions[None, :] < hist_len[:, None]
    event_bias = time_bias[time_bucket]
    user_ids = jnp.arange(USERS, dtype=jnp.int32)
    shard_keys = jnp.swapaxes(hist_keys.reshape(USERS, N_HIST, HL_DEV, D), 0, 1)
    shard_values = jnp.swapaxes(hist_values.reshape(USERS, N_HIST, HL_DEV, D), 0, 1)
    shard_bias = jnp.swapaxes(event_bias.reshape(USERS, N_HIST, HL_DEV, H), 0, 1)
    shard_live = jnp.swapaxes(key_live.reshape(USERS, N_HIST, HL_DEV), 0, 1)

    def one_user(total, inputs):
        user_keys, user_values, user_bias, user_live, user_id = inputs
        same_user = jnp.where((cand_user == user_id)[:, None] & user_live[None, :], 1.0, 0.0).astype(jnp.float32)
        head_outputs = []
        for head_index in range(H):
            first = head_index * DH
            logits = lax.dot_general(queries[:, first:first + DH], user_keys[:, first:first + DH], (((1,), (1,)), ((), ())), preferred_element_type=jnp.float32)
            logits = logits * score_scale + user_bias[:, head_index][None, :]
            weights_bf = (jax.nn.silu(logits) * same_user).astype(jnp.bfloat16)
            head_outputs.append(jnp.dot(weights_bf, user_values[:, first:first + DH], preferred_element_type=jnp.float32))
        return (total + jnp.concatenate(head_outputs, axis=1), None)

    def one_shard(total, inputs):
        keys_s, values_s, bias_s, live_s = inputs
        start_share = jnp.zeros((CANDS, D), jnp.float32)
        share, unused_inner = lax.scan(one_user, start_share, (keys_s, values_s, bias_s, live_s, user_ids))
        rounded = lax.optimization_barrier(share.astype(jnp.bfloat16))
        return (total + rounded.astype(jnp.float32), None)
    start_total = jnp.zeros((CANDS, D), jnp.float32)
    attended, unused = lax.scan(one_shard, start_total, (shard_keys, shard_values, shard_bias, shard_live))
    row_mean = lax.optimization_barrier(jnp.sum(attended, axis=1)) / D
    row_var = lax.optimization_barrier(jnp.sum(attended * attended, axis=1)) / D - row_mean * row_mean
    cand_states = ((attended - row_mean[:, None]) * lax.rsqrt(row_var[:, None] + 1e-05) * cand_gate.astype(jnp.float32)).astype(jnp.bfloat16)
    pre_act = jnp.dot(cand_states, tower_in, preferred_element_type=jnp.float32) + tower_bias[None, :]
    hidden = jax.nn.silu(pre_act)
    cand_scores = jnp.dot(hidden, tower_out, precision=lax.Precision.HIGHEST)
    return (cand_states, cand_scores)
```

```python
import functools

import jax
import jax.numpy as jnp
from jax import lax
from jax.experimental import pallas as pl
from jax.experimental.pallas import tpu as pltpu
from jax.sharding import PartitionSpec as P

DH = 128
CHUNKS = 2
MESH = pl.DeviceIdType.MESH
F32 = jnp.float32
BF16 = jnp.bfloat16


def partner_of(me, step, count):
    if count & (count - 1):
        return lax.rem(me + step, count)
    other, bit = 0, 1
    while bit < count:
        mine = lax.rem(me // bit, 2)
        other = other + (1 - mine if step & bit else mine) * bit
        bit *= 2
    return other


def source_of(me, step, count):
    if count & (count - 1):
        return lax.rem(me + count - step, count)
    return partner_of(me, step, count)


def kernel(
    n_hist,
    n_tower,
    q_hbm,
    k_hbm,
    v_hbm,
    user_hbm,
    bucket_hbm,
    len_hbm,
    gate_hbm,
    tbias_hbm,
    w_hbm,
    b_hbm,
    o_hbm,
    states_out,
    scores_out,
    q_own,
    q_all,
    u_all,
    k_buf,
    v_buf,
    bucket,
    len_ref,
    gate,
    tbias,
    w_buf,
    b_buf,
    o_buf,
    share_out,
    share_in,
    att_buf,
    score_send,
    score_in,
    load_sem,
    ready,
    pass_send,
    q_send,
    q_recv,
    u_send,
    u_recv,
    share_send,
    share_recv,
    w_send,
    w_recv,
    gate_send,
    gate_recv,
    att_send,
    att_recv,
    score_send_sem,
    score_recv,
):
    z = lax.axis_index("hist")
    x = lax.axis_index("tower")
    c = lax.axis_index("head")
    mate = 1 - c
    rows, feat = q_hbm.shape
    users, per_user, _ = k_hbm.shape
    hidden = b_buf.shape[1]
    total_feat = 2 * feat

    tower_peers = [(t, h) for t in range(n_tower) for h in range(2) if t or h]

    def tower_id(t, h):
        return {"tower": partner_of(x, t, n_tower), "head": mate if h else c}

    has_left, has_right = z > 0, z < n_hist - 1
    sides = ((has_left, z - 1), (has_right, z + 1))

    barrier = pltpu.get_barrier_semaphore()
    for exists, there in sides:

        @pl.when(exists)
        def _(there=there):
            pl.semaphore_signal(barrier, inc=1, device_id={"hist": there}, device_id_type=MESH)

    for t, h in tower_peers:
        pl.semaphore_signal(barrier, inc=1, device_id=tower_id(t, h), device_id_type=MESH)

    mine_cols = pl.ds(pl.multiple_of(c * hidden, 128), hidden)
    mate_cols = pl.ds(pl.multiple_of(mate * hidden, 128), hidden)
    loads = [
        pltpu.make_async_copy(src, dst, load_sem.at[i])
        for i, (src, dst) in enumerate(
            [
                (q_hbm, q_own),
                (user_hbm, u_all.at[z]),
                (bucket_hbm, bucket),
                (tbias_hbm, tbias),
                (k_hbm, k_buf),
                (v_hbm, v_buf),
                (gate_hbm, gate.at[x, c]),
                (b_hbm.at[:, mine_cols], b_buf),
                (o_hbm.at[:, mine_cols], o_buf),
                (w_hbm.at[:, mine_cols], w_buf.at[c]),
                (len_hbm, len_ref),
            ]
        )
    ]
    for load in loads:
        load.start()

    neighbours = has_left.astype(jnp.int32) + has_right.astype(jnp.int32)
    pl.semaphore_wait(barrier, neighbours + len(tower_peers))

    def remote(src, dst, send, recv, device_id):
        return pltpu.make_async_remote_copy(
            src_ref=src,
            dst_ref=dst,
            send_sem=send,
            recv_sem=recv,
            device_id=device_id,
            device_id_type=MESH,
        )

    chunks = q_all.shape[1]
    width = feat // chunks

    def query_copy(there, chunk):
        return remote(
            q_hbm.at[:, chunk * width : (chunk + 1) * width],
            q_all.at[z, chunk],
            q_send.at[there, chunk],
            q_recv.at[z, chunk],
            {"hist": there},
        )

    def user_copy(there):
        return remote(user_hbm, u_all.at[z], u_send.at[there], u_recv.at[z], {"hist": there})

    def each_other(action):
        for distance in range(1, n_hist):
            for sign, behind in ((-1, has_right), (1, has_left)):
                there = z + sign * distance
                pl.when((there >= 0) & (there < n_hist))(
                    functools.partial(action, distance, there, z - sign, behind)
                )

    def goes_direct(distance, behind):
        return jnp.logical_not(behind) if distance == 2 else z >= 0

    passes = (
        ((z >= 2) & (z + 1 < n_hist), z - 1, z + 1),
        ((z >= 1) & (z + 2 < n_hist), z + 1, z - 1),
    )

    def pass_copy(way, block, there, chunk):
        return remote(
            q_all.at[block, chunk],
            q_all.at[block, chunk],
            pass_send.at[way, chunk],
            q_recv.at[block, chunk],
            {"hist": there},
        )

    def send_queries(distance, there, back, behind):
        if distance > 1:
            pl.semaphore_wait(ready.at[there], 1)

        @pl.when(behind)
        def _():
            pl.semaphore_signal(
                ready.at[there], inc=1, device_id={"hist": back}, device_id_type=MESH
            )

        user_copy(there).start()

        @pl.when(goes_direct(distance, behind))
        def _():
            for chunk in range(chunks):
                query_copy(there, chunk).start()

    each_other(send_queries)
    sends = []
    w_copy = remote(
        w_hbm.at[:, mate_cols], w_buf.at[c], w_send.at[0], w_recv.at[0], {"head": mate}
    )
    w_copy.start()
    sends.append(w_copy)
    for i, (t, h) in enumerate(tower_peers):
        copy = remote(
            gate_hbm, gate.at[x, c], gate_send.at[i], gate_recv.at[x, c], tower_id(t, h)
        )
        copy.start()
        sends.append(copy)

    loads[2].wait()
    loads[3].wait()
    loads[10].wait()
    heads, bucket_count = tbias.shape
    half_scale = 0.5 * DH ** (-0.5)
    tb = tbias[...] * 0.5
    bias_rows, owner_rows = [], []
    for u in range(users):
        onehot = jnp.where(
            lax.broadcasted_iota(jnp.int32, (bucket_count, per_user), 0) == bucket[u : u + 1, :],
            1.0,
            0.0,
        ).astype(F32)
        bias_rows.append(
            lax.dot_general(
                tb,
                onehot,
                (((1,), (0,)), ((), ())),
                precision=lax.Precision.HIGHEST,
                preferred_element_type=F32,
            )
        )
        position = z * per_user + lax.broadcasted_iota(jnp.int32, (1, per_user), 1)
        owner_rows.append(jnp.where(position < len_ref[:, u : u + 1], u, -1))
    bias = jnp.concatenate(bias_rows, axis=1)
    owner = jnp.concatenate(owner_rows, axis=1)
    events = users * per_user

    loads[0].wait()
    loads[1].wait()
    loads[4].wait()
    loads[5].wait()

    def live_of(index):
        user_col = jnp.broadcast_to(u_all[index], (128, rows)).T[:, :1]
        return jnp.where(user_col == owner, 1.0, 0.0).astype(F32)

    def attend(query, live, head):
        cols = slice(head * DH, (head + 1) * DH)
        s = lax.dot_general(
            query,
            k_buf[:, :, cols].reshape(events, DH),
            (((1,), (1,)), ((), ())),
            preferred_element_type=F32,
        )
        half = s * half_scale + bias[head : head + 1, :]
        weight = ((half + half * jnp.tanh(half)) * live).astype(BF16)
        return jnp.dot(
            weight, v_buf[:, :, cols].reshape(events, DH), preferred_element_type=F32
        ).astype(BF16)

    per_chunk = heads // chunks
    own_live = live_of(z)
    for head in range(heads):
        cols = slice((head % per_chunk) * DH, (head % per_chunk + 1) * DH)
        share_in[z, head // per_chunk, :, cols] = attend(
            q_own[:, head * DH : (head + 1) * DH], own_live, head
        )

    nearer = jnp.minimum(z, n_hist - 1 - z)

    def block_at(step):
        distance = (step + 1) // 2
        paired = z - distance if step % 2 else z + distance
        rest = jnp.where(z < n_hist - 1 - z, z + step - nearer, z - step + nearer)
        return jnp.where(step <= 2 * nearer, paired, rest)

    def users_arrive(block):
        remote(
            user_hbm, u_all.at[block], u_send.at[block], u_recv.at[block], {"hist": block}
        ).wait_recv()

    def arrive(block, chunk):
        remote(
            q_hbm.at[:, 0:width],
            q_all.at[block, chunk],
            q_send.at[block, chunk],
            q_recv.at[block, chunk],
            {"hist": block},
        ).wait_recv()

    def share_copy(step, chunk):
        return remote(
            share_out.at[step, chunk],
            share_in.at[z, chunk],
            share_send.at[step, chunk],
            share_recv.at[z, chunk],
            {"hist": block_at(step)},
        )

    for chunk in range(chunks):
        for way, (passing, block, there) in enumerate(passes):

            @pl.when(passing)
            def _(way=way, block=block, there=there, chunk=chunk):
                arrive(block, chunk)
                pass_copy(way, block, there, chunk).start()

    for step in range(1, n_hist):
        block = block_at(step)
        taken = (passes[0][0] & (block == z - 1)) | (passes[1][0] & (block == z + 1))
        for chunk in range(chunks):
            if chunk == 0:
                users_arrive(block)

            @pl.when(jnp.logical_not(taken))
            def _(block=block, chunk=chunk):
                arrive(block, chunk)

            if chunk == 0:
                live = live_of(block)
            for i in range(per_chunk):
                cols = slice(i * DH, (i + 1) * DH)
                share_out[step, chunk, :, cols] = attend(
                    q_all[block, chunk, :, cols], live, chunk * per_chunk + i
                )
            copy = share_copy(step, chunk)
            copy.start()
            sends.append(copy)

    def share_arrives(src, chunk):
        remote(
            share_out.at[1, chunk],
            share_in.at[src, chunk],
            share_send.at[1, chunk],
            share_recv.at[src, chunk],
            {"hist": src},
        ).wait_recv()

    own = []
    for chunk in range(chunks):
        for step in range(1, n_hist):
            share_arrives(block_at(step), chunk)
        part = share_in[0, chunk].astype(F32)
        for s in range(1, n_hist):
            part = part + share_in[s, chunk].astype(F32)
        own.append(part)
        att_buf[x, c, chunk] = part.astype(BF16)
        for i, (t, h) in reversed(list(enumerate(tower_peers))):
            copy = remote(
                att_buf.at[x, c, chunk],
                att_buf.at[x, c, chunk],
                att_send.at[i, chunk],
                att_recv.at[x, c, chunk],
                tower_id(t, h),
            )
            copy.start()
            sends.append(copy)

    def half_arrives(tower, head):
        remote(
            gate_hbm, gate.at[tower, head], gate_send.at[0], gate_recv.at[tower, head], {"head": mate}
        ).wait_recv()
        for chunk in range(chunks):
            remote(
                att_buf.at[tower, head, chunk],
                att_buf.at[tower, head, chunk],
                att_send.at[0, chunk],
                att_recv.at[tower, head, chunk],
                {"head": mate},
            ).wait_recv()

    def half_of(tower, head):
        return [att_buf[tower, head, chunk].astype(F32) for chunk in range(chunks)]

    def normalised(pieces, gates):
        every = [p for half in pieces for p in half]
        row_sum = sum(jnp.sum(p, axis=1, keepdims=True) for p in every)
        row_squares = sum(jnp.sum(p * p, axis=1, keepdims=True) for p in every)
        row_mean = row_sum / total_feat
        row_var = row_squares / total_feat - row_mean * row_mean
        scale = lax.rsqrt(row_var + 1e-05)
        return [
            ((jnp.concatenate(half, axis=1) - row_mean) * scale * g.astype(F32)).astype(BF16)
            for half, g in zip(pieces, gates)
        ]

    loads[6].wait()
    loads[7].wait()
    loads[8].wait()
    loads[9].wait()
    remote(
        w_hbm.at[:, mate_cols], w_buf.at[mate], w_send.at[0], w_recv.at[0], {"head": mate}
    ).wait_recv()

    def scores_of(first, first_w, second, second_w):
        pre = jnp.dot(first, w_buf[first_w], preferred_element_type=F32)
        pre = pre + jnp.dot(second, w_buf[second_w], preferred_element_type=F32)
        half = (pre + b_buf[...]) * 0.5
        part = (half + half * jnp.tanh(half)) * o_buf[...]
        acc = part[:, 0:128]
        for i in range(1, hidden // 128):
            acc = acc + part[:, i * 128 : (i + 1) * 128]
        return jnp.broadcast_to(jnp.sum(acc.T, axis=0, keepdims=True), (8, rows))

    half_arrives(x, mate)
    mine, theirs = normalised([own, half_of(x, mate)], [gate[x, c], gate[x, mate]])
    states_out[...] = mine
    own_scores = scores_of(mine, c, theirs, mate)
    score_in[x, c] = own_scores
    copy = remote(
        score_in.at[x, c], score_in.at[x, c], score_send_sem.at[0], score_recv.at[x, c], {"head": mate}
    )
    copy.start()
    sends.append(copy)
    for t in range(1, n_tower):
        other = source_of(x, t, n_tower)
        half_arrives(other, c)
        half_arrives(other, mate)
        first, second = normalised(
            [half_of(other, 0), half_of(other, 1)], [gate[other, 0], gate[other, 1]]
        )
        score_send[t] = scores_of(first, 0, second, 1)
        for h in range(2):
            copy = remote(
                score_send.at[t],
                score_in.at[x, c],
                score_send_sem.at[2 * t + h],
                score_recv.at[x, c],
                {"tower": other, "head": mate if h else c},
            )
            copy.start()
            sends.append(copy)

    for t, h in tower_peers:
        tower, head = partner_of(x, t, n_tower), mate if h else c
        remote(
            score_in.at[tower, head],
            score_in.at[tower, head],
            score_send_sem.at[0],
            score_recv.at[tower, head],
            {"head": mate},
        ).wait_recv()
    total = score_in[0, 0] + score_in[0, 1]
    for t in range(1, n_tower):
        total = total + (score_in[t, 0] + score_in[t, 1])
    scores_out[...] = total[0:1, :]
    for copy in sends:
        copy.wait_send()

    def sent(distance, there, back, behind):
        user_copy(there).wait_send()

        @pl.when(goes_direct(distance, behind))
        def _():
            for chunk in range(chunks):
                query_copy(there, chunk).wait_send()

    each_other(sent)
    for way, (passing, block, there) in enumerate(passes):

        @pl.when(passing)
        def _(way=way, block=block, there=there):
            for chunk in range(chunks):
                pass_copy(way, block, there, chunk).wait_send()


def hand_over(states_in, scores_in, states_out, scores_out):
    states_out[...] = states_in[...]
    scores_out[...] = scores_in[...]


def local(
    queries,
    hist_keys,
    hist_values,
    cand_user,
    time_bucket,
    hist_len,
    cand_gate,
    time_bias,
    tower_in,
    tower_bias,
    tower_out,
    *,
    n_hist,
    n_tower,
):
    rows, feat = queries.shape
    hidden = tower_in.shape[1] // 2
    chunks = CHUNKS if (feat // DH) % CHUNKS == 0 else 1
    any_spec = pl.BlockSpec(memory_space=pl.ANY)
    vmem_spec = pl.BlockSpec(memory_space=pltpu.VMEM)
    dma = pltpu.SemaphoreType.DMA
    states, scores = pl.pallas_call(
        functools.partial(kernel, n_hist, n_tower),
        out_shape=(
            pltpu.VMEM((rows, feat), BF16),
            pltpu.VMEM((1, rows), F32),
        ),
        in_specs=[any_spec] * 11,
        out_specs=(vmem_spec, vmem_spec),
        scratch_shapes=[
            pltpu.VMEM((rows, feat), BF16),
            pltpu.VMEM((n_hist, chunks, rows, feat // chunks), BF16),
            pltpu.VMEM((n_hist, 1, rows), jnp.int32),
            pltpu.VMEM(hist_keys.shape, BF16),
            pltpu.VMEM(hist_values.shape, BF16),
            pltpu.VMEM(time_bucket.shape, jnp.int32),
            pltpu.VMEM((1,) + hist_len.shape, jnp.int32),
            pltpu.VMEM((n_tower, 2, rows, feat), BF16),
            pltpu.VMEM(time_bias.shape[::-1], F32),
            pltpu.VMEM((2, feat, hidden), BF16),
            pltpu.VMEM((1, hidden), F32),
            pltpu.VMEM((1, hidden), F32),
            pltpu.VMEM((n_hist, chunks, rows, feat // chunks), BF16),
            pltpu.VMEM((n_hist, chunks, rows, feat // chunks), BF16),
            pltpu.VMEM((n_tower, 2, chunks, rows, feat // chunks), BF16),
            pltpu.VMEM((n_tower, 8, rows), F32),
            pltpu.VMEM((n_tower, 2, 8, rows), F32),
            dma((11,)),
            pltpu.SemaphoreType.REGULAR((n_hist,)),
            dma((2, chunks)),
            dma((n_hist, chunks)),
            dma((n_hist, chunks)),
            dma((n_hist,)),
            dma((n_hist,)),
            dma((n_hist, chunks)),
            dma((n_hist, chunks)),
            dma((1,)),
            dma((1,)),
            dma((2 * n_tower,)),
            dma((n_tower, 2)),
            dma((2 * n_tower, chunks)),
            dma((n_tower, 2, chunks)),
            dma((2 * n_tower,)),
            dma((n_tower, 2)),
        ],
        compiler_params=pltpu.CompilerParams(collective_id=0, has_side_effects=True),
    )(
        queries,
        hist_keys,
        hist_values,
        cand_user.reshape(1, rows),
        time_bucket,
        hist_len.reshape(1, -1),
        cand_gate,
        time_bias.T,
        tower_in,
        tower_bias.reshape(1, -1),
        tower_out.reshape(1, -1),
    )
    states, scores = pl.pallas_call(
        hand_over,
        out_shape=(
            jax.ShapeDtypeStruct((rows, feat), BF16),
            jax.ShapeDtypeStruct((1, rows), F32),
        ),
        in_specs=[vmem_spec, vmem_spec],
        out_specs=(vmem_spec, vmem_spec),
    )(
        pltpu.with_memory_space_constraint(states, pltpu.VMEM),
        pltpu.with_memory_space_constraint(scores, pltpu.VMEM),
    )
    return states, scores.reshape(rows)


def solution(mesh):
    return jax.shard_map(
        functools.partial(local, n_hist=mesh.shape["hist"], n_tower=mesh.shape["tower"]),
        mesh=mesh,
        in_specs=(
            P(("groups", "hist", "tower"), "head"),
            P("groups", "hist", "head"),
            P("groups", "hist", "head"),
            P(("groups", "hist", "tower")),
            P("groups", "hist"),
            P("groups"),
            P(("groups", "hist", "tower"), "head"),
            P(None, "head"),
            P("head", "tower"),
            P("tower"),
            P("tower"),
        ),
        out_specs=(P(("groups", "hist", "tower"), "head"), P(("groups", "hist", "tower"))),
        check_vma=False,
    )
```

```python
import functools

import jax
import jax.numpy as jnp
from jax import lax
from jax.experimental import pallas as pl
from jax.experimental.pallas import tpu as pltpu
from jax.sharding import PartitionSpec as P

DH = 128
CHUNKS = 2
MESH = pl.DeviceIdType.MESH
F32 = jnp.float32
BF16 = jnp.bfloat16


def partner_of(me, step, count):
    if count & (count - 1):
        return lax.rem(me + step, count)
    other, bit = 0, 1
    while bit < count:
        mine = lax.rem(me // bit, 2)
        other = other + (1 - mine if step & bit else mine) * bit
        bit *= 2
    return other


def source_of(me, step, count):
    if count & (count - 1):
        return lax.rem(me + count - step, count)
    return partner_of(me, step, count)


def relayed(block, at, count):
    return abs(block - at) == 2 and block not in (0, count - 1)


def order_of(at, count):
    def key(block):
        handed_on = 0 <= 2 * at - block < count and relayed(block, 2 * at - block, count)
        hops = at - block if block < at else at + 0.6 * (block - at)
        return not (handed_on and abs(at - block) == 1), relayed(block, at, count), hops

    return sorted((b for b in range(count) if b != at), key=key)


def pick(me, values):
    if all(v == values[0] for v in values):
        return values[0]
    chosen = jnp.int32(values[0])
    for i, v in enumerate(values[1:], 1):
        chosen = jnp.where(me == i, jnp.int32(v), chosen)
    return chosen


def when(condition):
    if isinstance(condition, bool):
        return (lambda body: body()) if condition else (lambda body: None)
    return pl.when(condition)


def kernel(
    n_hist,
    n_tower,
    q_hbm,
    k_hbm,
    v_hbm,
    user_hbm,
    bucket_hbm,
    len_hbm,
    gate_hbm,
    tbias_hbm,
    w_hbm,
    b_hbm,
    o_hbm,
    states_out,
    scores_out,
    q_all,
    u_all,
    k_buf,
    v_buf,
    bucket,
    len_ref,
    gate,
    tbias,
    w_buf,
    b_buf,
    o_buf,
    own_share,
    share_out,
    share_in,
    att_buf,
    score_send,
    score_in,
    load_sem,
    q_load,
    above,
    peers,
    pass_send,
    pass_user_send,
    q_send,
    q_recv,
    u_send,
    u_recv,
    share_send,
    share_recv,
    w_send,
    w_recv,
    gate_send,
    gate_recv,
    att_send,
    att_recv,
    score_send_sem,
    score_recv,
):
    z = lax.axis_index("hist")
    x = lax.axis_index("tower")
    c = lax.axis_index("head")
    mate = 1 - c
    rows, feat = q_hbm.shape
    users, per_user, _ = k_hbm.shape
    hidden = b_buf.shape[1]
    total_feat = 2 * feat
    chunks = q_all.shape[1]
    width = feat // chunks

    tower_peers = [(t, h) for t in range(n_tower) for h in range(2) if t or h]

    def tower_id(t, h):
        return {"tower": partner_of(x, t, n_tower), "head": mate if h else c}

    def rank_of(tower, head):
        return 2 * tower + 1 - head

    rank = rank_of(x, c)
    peer_ranks = [
        (t, h, rank_of(partner_of(x, t, n_tower), mate if h else c)) for t, h in tower_peers
    ]
    barrier = pltpu.get_barrier_semaphore()
    for t, h, other_rank in peer_ranks:

        @pl.when(other_rank > rank)
        def _(t=t, h=h):
            pl.semaphore_signal(barrier, inc=1, device_id=tower_id(t, h), device_id_type=MESH)

    has_left, has_right = z > 0, z < n_hist - 1

    mine_cols = pl.ds(pl.multiple_of(c * hidden, 128), hidden)
    mate_cols = pl.ds(pl.multiple_of(mate * hidden, 128), hidden)
    q_loads = [
        pltpu.make_async_copy(q_hbm.at[:, i * width : (i + 1) * width], q_all.at[z, i], q_load)
        for i in range(chunks)
    ]
    loads = [
        pltpu.make_async_copy(src, dst, load_sem.at[i])
        for i, (src, dst) in enumerate(
            [
                (user_hbm, u_all.at[z]),
                (bucket_hbm, bucket),
                (tbias_hbm, tbias),
                (len_hbm, len_ref),
                (k_hbm, k_buf),
                (v_hbm, v_buf),
                (gate_hbm, gate.at[x, c]),
                (b_hbm.at[:, mine_cols], b_buf),
                (o_hbm.at[:, mine_cols], o_buf),
                (w_hbm.at[:, mine_cols], w_buf.at[c]),
            ]
        )
    ]
    user_load, bucket_load, tbias_load, len_load, k_load, v_load, *late_loads = loads
    for load in q_loads + loads[:6]:
        load.start()

    awaited = rank + has_left.astype(jnp.int32)

    @pl.when(awaited > 0)
    def _():
        pl.semaphore_wait(barrier, awaited)

    @pl.when(has_right)
    def _():
        pl.semaphore_signal(barrier, inc=1, device_id={"hist": z + 1}, device_id_type=MESH)

    for distance in range(1, n_hist):

        @pl.when(z >= distance)
        def _(distance=distance):
            pl.semaphore_signal(
                above.at[z], inc=1, device_id={"hist": z - distance}, device_id_type=MESH
            )

    for t, h, other_rank in peer_ranks:

        @pl.when(other_rank < rank)
        def _(t=t, h=h):
            pl.semaphore_signal(peers, inc=1, device_id=tower_id(t, h), device_id_type=MESH)

    def remote(src, dst, send, recv, device_id):
        return pltpu.make_async_remote_copy(
            src_ref=src,
            dst_ref=dst,
            send_sem=send,
            recv_sem=recv,
            device_id=device_id,
            device_id_type=MESH,
        )

    def query_copy(there, chunk):
        return remote(
            q_all.at[z, chunk],
            q_all.at[z, chunk],
            q_send.at[there],
            q_recv.at[z, chunk],
            {"hist": there},
        )

    def user_copy(there):
        return remote(u_all.at[z], u_all.at[z], u_send.at[there], u_recv.at[z], {"hist": there})

    def send_queries(there):
        user_copy(there).start()
        for chunk in range(chunks):
            query_copy(there, chunk).start()

    def goes_direct(distance, sign):
        if distance != 2:
            return True
        return z == 0 if sign > 0 else z == n_hist - 1

    def send_down(distance):
        @pl.when(z >= distance)
        def _():
            when(goes_direct(distance, -1))(lambda: send_queries(z - distance))

    def send_up(distance, condition):
        @pl.when(condition)
        def _():
            pl.semaphore_wait(above.at[z + distance], 1)
            when(goes_direct(distance, 1))(lambda: send_queries(z + distance))

    user_load.wait()
    pltpu.make_async_copy(q_all.at[z], q_all.at[z], q_load).wait()
    for distance in range(n_hist - 1, 0, -1):
        send_down(distance)

    send_up(1, z < n_hist - 2)

    bucket_load.wait()
    tbias_load.wait()
    len_load.wait()
    heads, bucket_count = tbias.shape
    half_scale = 0.5 * DH ** (-0.5)
    tb = tbias[...] * 0.5
    bias_rows, owner_rows = [], []
    for u in range(users):
        onehot = jnp.where(
            lax.broadcasted_iota(jnp.int32, (bucket_count, per_user), 0) == bucket[u : u + 1, :],
            1.0,
            0.0,
        ).astype(F32)
        bias_rows.append(
            lax.dot_general(
                tb,
                onehot,
                (((1,), (0,)), ((), ())),
                precision=lax.Precision.HIGHEST,
                preferred_element_type=F32,
            )
        )
        position = z * per_user + lax.broadcasted_iota(jnp.int32, (1, per_user), 1)
        owner_rows.append(jnp.where(position < len_ref[:, u : u + 1], u, -1))
    bias = jnp.concatenate(bias_rows, axis=1)
    owner = jnp.concatenate(owner_rows, axis=1)
    events = users * per_user
    k_load.wait()
    v_load.wait()

    def live_of(index):
        user_col = jnp.broadcast_to(u_all[index], (128, rows)).T[:, :1]
        return jnp.where(user_col == owner, 1.0, 0.0).astype(F32)

    def attend(query, live, head):
        cols = slice(head * DH, (head + 1) * DH)
        s = lax.dot_general(
            query,
            k_buf[:, :, cols].reshape(events, DH),
            (((1,), (1,)), ((), ())),
            preferred_element_type=F32,
        )
        half = s * half_scale + bias[head : head + 1, :]
        weight = ((half + half * jnp.tanh(half)) * live).astype(BF16)
        return jnp.dot(
            weight, v_buf[:, :, cols].reshape(events, DH), preferred_element_type=F32
        )

    per_chunk = heads // chunks

    def share_of(block, live, chunk):
        parts = [
            attend(q_all[block, chunk, :, i * DH : (i + 1) * DH], live, chunk * per_chunk + i)
            for i in range(per_chunk)
        ]
        return jnp.concatenate(parts, axis=1) if per_chunk > 1 else parts[0]

    own_live = live_of(z)
    for chunk in range(chunks):
        own_share[chunk] = share_of(z, own_live, chunk)

    for load in late_loads:
        load.start()

    send_up(1, z == n_hist - 2)
    for distance in range(2, n_hist):
        send_up(distance, z + distance < n_hist)


    @pl.when(rank < 2 * n_tower - 1)
    def _():
        pl.semaphore_wait(peers, 2 * n_tower - 1 - rank)
    sends = []
    w_copy = remote(
        w_hbm.at[:, mate_cols], w_buf.at[c], w_send.at[0], w_recv.at[0], {"head": mate}
    )
    w_copy.start()
    sends.append(w_copy)
    for i, (t, h) in enumerate(tower_peers):
        copy = remote(
            gate_hbm, gate.at[x, c], gate_send.at[i], gate_recv.at[x, c], tower_id(t, h)
        )
        copy.start()
        sends.append(copy)

    def user_arrives(block):
        remote(
            u_all.at[block], u_all.at[block], u_send.at[0], u_recv.at[block], {"hist": block}
        ).wait_recv()

    def query_arrives(block, chunk):
        remote(
            q_all.at[block, chunk],
            q_all.at[block, chunk],
            q_send.at[0],
            q_recv.at[block, chunk],
            {"hist": block},
        ).wait_recv()

    def pass_copy(step, block, there, chunk):
        return remote(
            q_all.at[block, chunk],
            q_all.at[block, chunk],
            pass_send.at[step],
            q_recv.at[block, chunk],
            {"hist": there},
        )

    def pass_user(step, block, there):
        return remote(
            u_all.at[block],
            u_all.at[block],
            pass_user_send.at[step],
            u_recv.at[block],
            {"hist": there},
        )

    def share_copy(step, chunk):
        return remote(
            share_out.at[step, chunk],
            share_in.at[z, chunk],
            share_send.at[step],
            share_recv.at[z, chunk],
            {"hist": steps[step][0]},
        )

    def flag(values):
        chosen = pick(z, [int(v) for v in values])
        return bool(chosen) if isinstance(chosen, int) else chosen == 1

    orders = [order_of(i, n_hist) for i in range(n_hist)]
    steps = []
    for step in range(n_hist - 1):
        blocks = [order[step] for order in orders]
        onward = [2 * i - b for i, b in enumerate(blocks)]
        hands_on = [
            abs(i - b) == 1 and 0 <= e < n_hist and relayed(b, e, n_hist)
            for i, (b, e) in enumerate(zip(blocks, onward))
        ]
        targets = [e if on else 0 for e, on in zip(onward, hands_on)]
        steps.append((pick(z, blocks), flag(hands_on), pick(z, targets)))

    for step, (block, passing, there) in enumerate(steps):
        user_arrives(block)

        @when(passing)
        def _():
            pass_user(step, block, there).start()

        live = live_of(block)
        holding = not passing if isinstance(passing, bool) else jnp.logical_not(passing)

        @when(passing)
        def _():
            for chunk in range(chunks):
                query_arrives(block, chunk)
                pass_copy(step, block, there, chunk).start()

        for chunk in range(chunks):
            @when(holding)
            def _():
                query_arrives(block, chunk)

            share_out[step, chunk] = share_of(block, live, chunk).astype(BF16)
            share_copy(step, chunk).start()

    sources = [block for block, _, _ in steps]

    own = []
    for chunk in range(chunks):
        for src in sources:
            remote(
                share_out.at[0, chunk],
                share_in.at[src, chunk],
                share_send.at[0],
                share_recv.at[src, chunk],
                {"hist": src},
            ).wait_recv()
        part = own_share[chunk]
        for src in sources:
            part = part + share_in[src, chunk].astype(F32)
        own.append(part)
        att_buf[x, c, chunk] = part.astype(BF16)
        for i, (t, h) in reversed(list(enumerate(tower_peers))):
            copy = remote(
                att_buf.at[x, c, chunk],
                att_buf.at[x, c, chunk],
                att_send.at[i],
                att_recv.at[x, c, chunk],
                tower_id(t, h),
            )
            copy.start()

    def half_arrives(tower, head):
        remote(
            gate_hbm, gate.at[tower, head], gate_send.at[0], gate_recv.at[tower, head], {"head": mate}
        ).wait_recv()
        for chunk in range(chunks):
            remote(
                att_buf.at[tower, head, chunk],
                att_buf.at[tower, head, chunk],
                att_send.at[0],
                att_recv.at[tower, head, chunk],
                {"head": mate},
            ).wait_recv()

    def half_of(tower, head):
        return [att_buf[tower, head, chunk].astype(F32) for chunk in range(chunks)]

    def normalised(pieces, gates):
        every = [p for half in pieces for p in half]
        row_sum = sum(jnp.sum(p, axis=1, keepdims=True) for p in every)
        row_squares = sum(jnp.sum(p * p, axis=1, keepdims=True) for p in every)
        row_mean = row_sum / total_feat
        row_var = row_squares / total_feat - row_mean * row_mean
        scale = lax.rsqrt(row_var + 1e-05)
        return [
            ((jnp.concatenate(half, axis=1) - row_mean) * scale * g.astype(F32)).astype(BF16)
            for half, g in zip(pieces, gates)
        ]

    for load in late_loads:
        load.wait()
    remote(
        w_hbm.at[:, mate_cols], w_buf.at[mate], w_send.at[0], w_recv.at[0], {"head": mate}
    ).wait_recv()

    def scores_of(first, first_w, second, second_w):
        pre = jnp.dot(first, w_buf[first_w], preferred_element_type=F32)
        pre = pre + jnp.dot(second, w_buf[second_w], preferred_element_type=F32)
        half = (pre + b_buf[...]) * 0.5
        part = (half + half * jnp.tanh(half)) * o_buf[...]
        acc = part[:, 0:128]
        for i in range(1, hidden // 128):
            acc = acc + part[:, i * 128 : (i + 1) * 128]
        return jnp.sum(acc.T, axis=0, keepdims=True)

    half_arrives(x, mate)
    mine, theirs = normalised([own, half_of(x, mate)], [gate[x, c], gate[x, mate]])
    states_out[...] = mine
    own_scores = scores_of(mine, c, theirs, mate)
    score_in[x, c] = own_scores
    copy = remote(
        score_in.at[x, c], score_in.at[x, c], score_send_sem.at[0], score_recv.at[x, c], {"head": mate}
    )
    copy.start()
    sends.append(copy)
    for t in range(1, n_tower):
        other = source_of(x, t, n_tower)
        half_arrives(other, c)
        half_arrives(other, mate)
        first, second = normalised(
            [half_of(other, 0), half_of(other, 1)], [gate[other, 0], gate[other, 1]]
        )
        score_send[t] = scores_of(first, 0, second, 1)
        for h in range(2):
            copy = remote(
                score_send.at[t],
                score_in.at[x, c],
                score_send_sem.at[2 * t + h],
                score_recv.at[x, c],
                {"tower": other, "head": mate if h else c},
            )
            copy.start()
            sends.append(copy)

    for t, h in tower_peers:
        tower, head = partner_of(x, t, n_tower), mate if h else c
        remote(
            score_in.at[tower, head],
            score_in.at[tower, head],
            score_send_sem.at[0],
            score_recv.at[tower, head],
            {"head": mate},
        ).wait_recv()
    total = score_in[0, 0] + score_in[0, 1]
    for t in range(1, n_tower):
        total = total + (score_in[t, 0] + score_in[t, 1])
    scores_out[...] = total
    for copy in sends:
        copy.wait_send()
    for i, (t, h) in enumerate(tower_peers):
        remote(
            att_buf.at[x, c], att_buf.at[x, c], att_send.at[i], att_recv.at[x, c, 0], tower_id(t, h)
        ).wait_send()
    for step, (block, passing, there) in enumerate(steps):
        remote(
            share_out.at[step], share_in.at[z], share_send.at[step], share_recv.at[z, 0], {"hist": block}
        ).wait_send()

        @when(passing)
        def _():
            pass_user(step, block, there).wait_send()
            remote(
                q_all.at[block], q_all.at[block], pass_send.at[step], q_recv.at[block, 0], {"hist": there}
            ).wait_send()

    def sent(there):
        user_copy(there).wait_send()
        remote(
            q_all.at[z], q_all.at[z], q_send.at[there], q_recv.at[z, 0], {"hist": there}
        ).wait_send()

    for distance in range(1, n_hist):
        for sign, exists in ((-1, z >= distance), (1, z + distance < n_hist)):

            @pl.when(exists)
            def _(distance=distance, sign=sign):
                when(goes_direct(distance, sign))(lambda: sent(z + sign * distance))


def hand_over(states_in, scores_in, states_out, scores_out):
    states_out[...] = states_in[...]
    scores_out[...] = scores_in[...]


def local(
    queries,
    hist_keys,
    hist_values,
    cand_user,
    time_bucket,
    hist_len,
    cand_gate,
    time_bias,
    tower_in,
    tower_bias,
    tower_out,
    *,
    n_hist,
    n_tower,
):
    rows, feat = queries.shape
    hidden = tower_in.shape[1] // 2
    chunks = CHUNKS if (feat // DH) % CHUNKS == 0 else 1
    width = feat // chunks
    any_spec = pl.BlockSpec(memory_space=pl.ANY)
    vmem_spec = pl.BlockSpec(memory_space=pltpu.VMEM)
    dma = pltpu.SemaphoreType.DMA
    states, scores = pl.pallas_call(
        functools.partial(kernel, n_hist, n_tower),
        out_shape=(
            pltpu.VMEM((rows, feat), BF16),
            pltpu.VMEM((1, rows), F32),
        ),
        in_specs=[any_spec] * 11,
        out_specs=(vmem_spec, vmem_spec),
        scratch_shapes=[
            pltpu.VMEM((n_hist, chunks, rows, width), BF16),
            pltpu.VMEM((n_hist, 1, rows), jnp.int32),
            pltpu.VMEM(hist_keys.shape, BF16),
            pltpu.VMEM(hist_values.shape, BF16),
            pltpu.VMEM(time_bucket.shape, jnp.int32),
            pltpu.VMEM((1,) + hist_len.shape, jnp.int32),
            pltpu.VMEM((n_tower, 2, rows, feat), BF16),
            pltpu.VMEM(time_bias.shape[::-1], F32),
            pltpu.VMEM((2, feat, hidden), BF16),
            pltpu.VMEM((1, hidden), F32),
            pltpu.VMEM((1, hidden), F32),
            pltpu.VMEM((chunks, rows, width), F32),
            pltpu.VMEM((n_hist, chunks, rows, width), BF16),
            pltpu.VMEM((n_hist, chunks, rows, width), BF16),
            pltpu.VMEM((n_tower, 2, chunks, rows, width), BF16),
            pltpu.VMEM((n_tower, 1, rows), F32),
            pltpu.VMEM((n_tower, 2, 1, rows), F32),
            dma((10,)),
            dma,
            pltpu.SemaphoreType.REGULAR((n_hist,)),
            pltpu.SemaphoreType.REGULAR,
            dma((n_hist - 1,)),
            dma((n_hist - 1,)),
            dma((n_hist,)),
            dma((n_hist, chunks)),
            dma((n_hist,)),
            dma((n_hist,)),
            dma((n_hist - 1,)),
            dma((n_hist, chunks)),
            dma((1,)),
            dma((1,)),
            dma((2 * n_tower - 1,)),
            dma((n_tower, 2)),
            dma((2 * n_tower - 1,)),
            dma((n_tower, 2, chunks)),
            dma((2 * n_tower,)),
            dma((n_tower, 2)),
        ],
        compiler_params=pltpu.CompilerParams(collective_id=0, has_side_effects=True),
    )(
        queries,
        hist_keys,
        hist_values,
        cand_user.reshape(1, rows),
        time_bucket,
        hist_len.reshape(1, -1),
        cand_gate,
        time_bias.T,
        tower_in,
        tower_bias.reshape(1, -1),
        tower_out.reshape(1, -1),
    )
    states, scores = pl.pallas_call(
        hand_over,
        out_shape=(
            jax.ShapeDtypeStruct((rows, feat), BF16),
            jax.ShapeDtypeStruct((1, rows), F32),
        ),
        in_specs=[vmem_spec, vmem_spec],
        out_specs=(vmem_spec, vmem_spec),
    )(
        pltpu.with_memory_space_constraint(states, pltpu.VMEM),
        pltpu.with_memory_space_constraint(scores, pltpu.VMEM),
    )
    return states, scores.reshape(rows)


def solution(mesh):
    return jax.shard_map(
        functools.partial(local, n_hist=mesh.shape["hist"], n_tower=mesh.shape["tower"]),
        mesh=mesh,
        in_specs=(
            P(("groups", "hist", "tower"), "head"),
            P("groups", "hist", "head"),
            P("groups", "hist", "head"),
            P(("groups", "hist", "tower")),
            P("groups", "hist"),
            P("groups"),
            P(("groups", "hist", "tower"), "head"),
            P(None, "head"),
            P("head", "tower"),
            P("tower"),
            P("tower"),
        ),
        out_specs=(P(("groups", "hist", "tower"), "head"), P(("groups", "hist", "tower"))),
        check_vma=False,
    )
```

```python
import functools

import jax
import jax.numpy as jnp
from jax import lax
from jax.experimental import pallas as pl
from jax.experimental.pallas import tpu as pltpu
from jax.sharding import PartitionSpec as P

DH = 128
CHUNKS = 2
MESH = pl.DeviceIdType.MESH
F32 = jnp.float32
BF16 = jnp.bfloat16


def partner_of(me, step, count):
    if count & (count - 1):
        return lax.rem(me + step, count)
    other, bit = 0, 1
    while bit < count:
        mine = lax.rem(me // bit, 2)
        other = other + (1 - mine if step & bit else mine) * bit
        bit *= 2
    return other


def source_of(me, step, count):
    if count & (count - 1):
        return lax.rem(me + count - step, count)
    return partner_of(me, step, count)


def relayed(block, at, count):
    return abs(block - at) == 2 and block not in (0, count - 1)


def order_of(at, count):
    def key(block):
        handed_on = 0 <= 2 * at - block < count and relayed(block, 2 * at - block, count)
        hops = at - block if block < at else at + 0.6 * (block - at)
        return at <= 1 and block, not (handed_on and abs(at - block) == 1), relayed(block, at, count), hops

    return sorted((b for b in range(count) if b != at), key=key)


def pick(me, values):
    if all(v == values[0] for v in values):
        return values[0]
    chosen = jnp.int32(values[0])
    for i, v in enumerate(values[1:], 1):
        chosen = jnp.where(me == i, jnp.int32(v), chosen)
    return chosen


def when(condition):
    if isinstance(condition, bool):
        return (lambda body: body()) if condition else (lambda body: None)
    return pl.when(condition)


def kernel(
    n_hist,
    n_tower,
    q_hbm,
    k_hbm,
    v_hbm,
    user_hbm,
    bucket_hbm,
    len_hbm,
    gate_hbm,
    tbias_hbm,
    w_hbm,
    b_hbm,
    o_hbm,
    states_out,
    scores_out,
    q_all,
    u_all,
    k_buf,
    v_buf,
    bucket,
    len_ref,
    gate,
    tbias,
    w_buf,
    b_buf,
    o_buf,
    own_share,
    share_out,
    share_in,
    att_buf,
    score_send,
    score_in,
    load_sem,
    q_load,
    above,
    peers,
    q_send,
    q_recv,
    u_send,
    u_recv,
    share_send,
    share_recv,
    w_send,
    w_recv,
    gate_send,
    gate_recv,
    att_send,
    att_recv,
    score_send_sem,
    score_recv,
):
    z = lax.axis_index("hist")
    x = lax.axis_index("tower")
    c = lax.axis_index("head")
    mate = 1 - c
    rows, feat = q_hbm.shape
    users, per_user, _ = k_hbm.shape
    hidden = b_buf.shape[1]
    total_feat = 2 * feat
    chunks = q_all.shape[1]
    width = feat // chunks

    tower_peers = [(t, h) for t in range(n_tower) for h in range(2) if t or h]

    def tower_id(t, h):
        return {"tower": partner_of(x, t, n_tower), "head": mate if h else c}

    def rank_of(tower, head):
        return 2 * tower + 1 - head

    rank = rank_of(x, c)
    peer_ranks = [
        (t, h, rank_of(partner_of(x, t, n_tower), mate if h else c)) for t, h in tower_peers
    ]
    barrier = pltpu.get_barrier_semaphore()
    for t, h, other_rank in peer_ranks:

        @pl.when(other_rank > rank)
        def _(t=t, h=h):
            pl.semaphore_signal(barrier, inc=1, device_id=tower_id(t, h), device_id_type=MESH)

    has_left, has_right = z > 0, z < n_hist - 1

    mine_cols = pl.ds(pl.multiple_of(c * hidden, 128), hidden)
    mate_cols = pl.ds(pl.multiple_of(mate * hidden, 128), hidden)
    q_loads = [
        pltpu.make_async_copy(q_hbm.at[:, i * width : (i + 1) * width], q_all.at[z, i], q_load)
        for i in range(chunks)
    ]
    loads = [
        pltpu.make_async_copy(src, dst, load_sem.at[i])
        for i, (src, dst) in enumerate(
            [
                (user_hbm, u_all.at[z]),
                (bucket_hbm, bucket),
                (tbias_hbm, tbias),
                (len_hbm, len_ref),
                (k_hbm, k_buf),
                (v_hbm, v_buf),
                (gate_hbm, gate.at[2 * x + c]),
                (b_hbm.at[:, mine_cols], b_buf),
                (o_hbm.at[:, mine_cols], o_buf),
                (w_hbm.at[:, mine_cols], w_buf.at[c]),
            ]
        )
    ]
    user_load, bucket_load, tbias_load, len_load, k_load, v_load, *late_loads = loads
    for load in q_loads + loads[:6]:
        load.start()

    awaited = rank + has_left.astype(jnp.int32)

    @pl.when(awaited > 0)
    def _():
        pl.semaphore_wait(barrier, awaited)

    @pl.when(has_right)
    def _():
        pl.semaphore_signal(barrier, inc=1, device_id={"hist": z + 1}, device_id_type=MESH)

    for distance in range(1, n_hist):

        @pl.when(z >= distance)
        def _(distance=distance):
            pl.semaphore_signal(
                above.at[z], inc=1, device_id={"hist": z - distance}, device_id_type=MESH
            )

    for t, h, other_rank in peer_ranks:

        @pl.when(other_rank < rank)
        def _(t=t, h=h):
            pl.semaphore_signal(peers, inc=1, device_id=tower_id(t, h), device_id_type=MESH)

    def remote(src, dst, send, recv, device_id):
        return pltpu.make_async_remote_copy(
            src_ref=src,
            dst_ref=dst,
            send_sem=send,
            recv_sem=recv,
            device_id=device_id,
            device_id_type=MESH,
        )

    def query_copy(there, chunk):
        return remote(
            q_all.at[z, chunk],
            q_all.at[z, chunk],
            q_send,
            q_recv.at[z, chunk],
            {"hist": there},
        )

    def user_copy(there):
        return remote(u_all.at[z], u_all.at[z], u_send, u_recv.at[z], {"hist": there})

    def send_queries(there):
        user_copy(there).start()
        for chunk in range(chunks):
            query_copy(there, chunk).start()

    def goes_direct(distance, sign):
        if distance != 2:
            return True
        return z == 0 if sign > 0 else z == n_hist - 1

    def send_down(distance):
        @pl.when(z >= distance)
        def _():
            when(goes_direct(distance, -1))(lambda: send_queries(z - distance))

    def send_up(distance, condition):
        @pl.when(condition)
        def _():
            pl.semaphore_wait(above.at[z + distance], 1)
            when(goes_direct(distance, 1))(lambda: send_queries(z + distance))

    user_load.wait()
    pltpu.make_async_copy(q_all.at[z], q_all.at[z], q_load).wait()
    for distance in range(n_hist - 1, 0, -1):
        send_down(distance)

    send_up(1, z < n_hist - 2)

    bucket_load.wait()
    tbias_load.wait()
    len_load.wait()
    heads, bucket_count = tbias.shape
    half_scale = 0.5 * DH ** (-0.5)
    tb = tbias[...] * 0.5
    bias_rows, owner_rows = [], []
    for u in range(users):
        onehot = jnp.where(
            lax.broadcasted_iota(jnp.int32, (bucket_count, per_user), 0) == bucket[u : u + 1, :],
            1.0,
            0.0,
        ).astype(F32)
        bias_rows.append(
            lax.dot_general(
                tb,
                onehot,
                (((1,), (0,)), ((), ())),
                precision=lax.Precision.HIGHEST,
                preferred_element_type=F32,
            )
        )
        position = z * per_user + lax.broadcasted_iota(jnp.int32, (1, per_user), 1)
        owner_rows.append(jnp.where(position < len_ref[:, u : u + 1], u, -1))
    bias = jnp.concatenate(bias_rows, axis=1)
    owner = jnp.concatenate(owner_rows, axis=1)
    events = users * per_user
    k_load.wait()
    v_load.wait()

    def live_of(index):
        user_col = jnp.broadcast_to(u_all[index], (128, rows)).T[:, :1]
        return jnp.where(user_col == owner, 1.0, 0.0).astype(F32)

    def scored(query, head):
        cols = slice(head * DH, (head + 1) * DH)
        return lax.dot_general(
            query,
            k_buf[:, :, cols].reshape(events, DH),
            (((1,), (1,)), ((), ())),
            preferred_element_type=F32,
        )

    def weighed(s, live, head):
        half = s * half_scale + bias[head : head + 1, :]
        return ((half + half * jnp.tanh(half)) * live).astype(BF16)

    def gathered(weight, head):
        cols = slice(head * DH, (head + 1) * DH)
        return jnp.dot(
            weight, v_buf[:, :, cols].reshape(events, DH), preferred_element_type=F32
        )

    per_chunk = heads // chunks

    def share_of(block, live, chunk):
        mine = [chunk * per_chunk + i for i in range(per_chunk)]
        s = [scored(q_all[block, chunk, :, i * DH : (i + 1) * DH], head) for i, head in enumerate(mine)]
        weights = [weighed(s[i], live, head) for i, head in enumerate(mine)]
        parts = [gathered(weights[i], head) for i, head in enumerate(mine)]
        return jnp.concatenate(parts, axis=1) if per_chunk > 1 else parts[0]

    own_live = live_of(z)
    for chunk in range(chunks):
        own_share[chunk] = share_of(z, own_live, chunk)

    for load in late_loads:
        load.start()

    send_up(1, z == n_hist - 2)
    for distance in range(2, n_hist):
        send_up(distance, z + distance < n_hist)


    @pl.when(rank < 2 * n_tower - 1)
    def _():
        pl.semaphore_wait(peers, 2 * n_tower - 1 - rank)
    w_copy = remote(
        w_hbm.at[:, mate_cols], w_buf.at[c], w_send.at[0], w_recv.at[0], {"head": mate}
    )
    w_copy.start()
    for i, (t, h) in enumerate(tower_peers):
        copy = remote(
            gate_hbm, gate.at[2 * x + c], gate_send, gate_recv.at[2 * x + c], tower_id(t, h)
        )
        copy.start()

    def user_arrives(block):
        remote(
            u_all.at[block], u_all.at[block], u_send, u_recv.at[block], {"hist": block}
        ).wait_recv()

    def query_arrives(block, chunk):
        remote(
            q_all.at[block, chunk],
            q_all.at[block, chunk],
            q_send,
            q_recv.at[block, chunk],
            {"hist": block},
        ).wait_recv()

    def pass_copy(step, block, there, chunk):
        return remote(
            q_all.at[block, chunk],
            q_all.at[block, chunk],
            q_send,
            q_recv.at[block, chunk],
            {"hist": there},
        )

    def pass_user(step, block, there):
        return remote(
            u_all.at[block],
            u_all.at[block],
            u_send,
            u_recv.at[block],
            {"hist": there},
        )

    def share_copy(step, chunk):
        return remote(
            share_out.at[step, chunk],
            share_in.at[z, chunk],
            share_send,
            share_recv.at[z, chunk],
            {"hist": steps[step][0]},
        )

    def flag(values):
        chosen = pick(z, [int(v) for v in values])
        return bool(chosen) if isinstance(chosen, int) else chosen == 1

    orders = [order_of(i, n_hist) for i in range(n_hist)]
    steps = []
    for step in range(n_hist - 1):
        blocks = [order[step] for order in orders]
        onward = [2 * i - b for i, b in enumerate(blocks)]
        hands_on = [
            abs(i - b) == 1 and 0 <= e < n_hist and relayed(b, e, n_hist)
            for i, (b, e) in enumerate(zip(blocks, onward))
        ]
        targets = [e if on else 0 for e, on in zip(onward, hands_on)]
        steps.append((pick(z, blocks), flag(hands_on), pick(z, targets)))

    for step, (block, passing, there) in enumerate(steps):
        user_arrives(block)

        @when(passing)
        def _():
            pass_user(step, block, there).start()

        live = live_of(block)
        holding = not passing if isinstance(passing, bool) else jnp.logical_not(passing)

        @when(passing)
        def _():
            for chunk in range(chunks):
                query_arrives(block, chunk)
                pass_copy(step, block, there, chunk).start()

        for chunk in range(chunks):
            @when(holding)
            def _():
                query_arrives(block, chunk)

            share_out[step, chunk] = share_of(block, live, chunk).astype(BF16)
            share_copy(step, chunk).start()

    sources = [block for block, _, _ in steps]

    def att_copy(tower, head, chunk, device_id):
        return remote(
            att_buf.at[2 * tower + head, chunk],
            att_buf.at[2 * tower + head, chunk],
            att_send,
            att_recv.at[2 * tower + head],
            device_id,
        )

    own = []
    for chunk in range(chunks):
        for src in sources:
            remote(
                share_out.at[0, chunk],
                share_in.at[src, chunk],
                share_send,
                share_recv.at[src, chunk],
                {"hist": src},
            ).wait_recv()
        part = own_share[chunk]
        for src in sources:
            part = part + share_in[src, chunk].astype(F32)
        own.append(part)
        att_buf[2 * x + c, chunk] = part.astype(BF16)
        for t in range(1, n_tower):
            for head in range(2):
                att_copy(x, c, chunk, {"tower": partner_of(x, t, n_tower), "head": head}).start()
        att_copy(x, c, chunk, {"head": mate}).start()

    def half_arrives(tower, head):
        remote(
            gate_hbm, gate.at[2 * tower + head], gate_send, gate_recv.at[2 * tower + head], {"head": mate}
        ).wait_recv()
        remote(
            att_buf.at[2 * tower + head],
            att_buf.at[2 * tower + head],
            att_send,
            att_recv.at[2 * tower + head],
            {"head": mate},
        ).wait_recv()

    def half_of(tower, head):
        return [att_buf[2 * tower + head, chunk].astype(F32) for chunk in range(chunks)]

    def normalised(pieces, gates):
        every = [p for half in pieces for p in half]
        row_sum = sum(jnp.sum(p, axis=1, keepdims=True) for p in every)
        row_squares = sum(jnp.sum(p * p, axis=1, keepdims=True) for p in every)
        row_mean = row_sum / total_feat
        row_var = row_squares / total_feat - row_mean * row_mean
        scale = lax.rsqrt(row_var + 1e-05)
        return [
            ((jnp.concatenate(half, axis=1) - row_mean) * scale * g.astype(F32)).astype(BF16)
            for half, g in zip(pieces, gates)
        ]

    for load in late_loads:
        load.wait()
    remote(
        w_hbm.at[:, mate_cols], w_buf.at[mate], w_send.at[0], w_recv.at[0], {"head": mate}
    ).wait_recv()

    def scores_of(first, first_w, second, second_w):
        pre = jnp.dot(first, w_buf[first_w], preferred_element_type=F32)
        pre = pre + jnp.dot(second, w_buf[second_w], preferred_element_type=F32)
        half = (pre + b_buf[...]) * 0.5
        part = (half + half * jnp.tanh(half)) * o_buf[...]
        acc = part[:, 0:128]
        for i in range(1, hidden // 128):
            acc = acc + part[:, i * 128 : (i + 1) * 128]
        return jnp.sum(acc.T, axis=0, keepdims=True)

    half_arrives(x, mate)
    mine, theirs = normalised([own, half_of(x, mate)], [gate[2 * x + c], gate[2 * x + mate]])
    states_out[...] = mine
    own_scores = scores_of(mine, c, theirs, mate)
    score_in[2 * x + c] = own_scores
    copy = remote(
        score_in.at[2 * x + c], score_in.at[2 * x + c], score_send_sem, score_recv.at[2 * x + c], {"head": mate}
    )
    copy.start()
    for t in range(1, n_tower):
        other = source_of(x, t, n_tower)
        half_arrives(other, c)
        half_arrives(other, mate)
        first, second = normalised(
            [half_of(other, 0), half_of(other, 1)], [gate[2 * other], gate[2 * other + 1]]
        )
        score_send[t] = scores_of(first, 0, second, 1)
        for h in range(2):
            copy = remote(
                score_send.at[t],
                score_in.at[2 * x + c],
                score_send_sem,
                score_recv.at[2 * x + c],
                {"tower": other, "head": h},
            )
            copy.start()

    for t, h in tower_peers:
        tower, head = partner_of(x, t, n_tower), mate if h else c
        remote(
            score_in.at[2 * tower + head],
            score_in.at[2 * tower + head],
            score_send_sem,
            score_recv.at[2 * tower + head],
            {"head": mate},
        ).wait_recv()
    total = score_in[0] + score_in[1]
    for t in range(1, n_tower):
        total = total + (score_in[2 * t] + score_in[2 * t + 1])
    scores_out[...] = total
    w_copy.wait_send()
    others, peer_count = slice(0, n_hist - 1), slice(0, 2 * n_tower - 1)
    for ref, send, recv in (
        (q_all.at[others], q_send, q_recv.at[0, 0]),
        (u_all.at[others], u_send, u_recv.at[0]),
        (share_out.at[others], share_send, share_recv.at[0, 0]),
        (gate.at[peer_count], gate_send, gate_recv.at[0]),
        (att_buf.at[peer_count], att_send, att_recv.at[0]),
        (score_in.at[peer_count], score_send_sem, score_recv.at[0]),
    ):
        remote(ref, ref, send, recv, {"head": mate}).wait_send()


def hand_over(states_in, scores_in, states_out, scores_out, sems):
    copies = [
        pltpu.make_async_copy(states_in, states_out, sems.at[0]),
        pltpu.make_async_copy(scores_in, scores_out, sems.at[1]),
    ]
    for copy in copies:
        copy.start()
    for copy in copies:
        copy.wait()


def local(
    queries,
    hist_keys,
    hist_values,
    cand_user,
    time_bucket,
    hist_len,
    cand_gate,
    time_bias,
    tower_in,
    tower_bias,
    tower_out,
    *,
    n_hist,
    n_tower,
):
    rows, feat = queries.shape
    hidden = tower_in.shape[1] // 2
    chunks = CHUNKS if (feat // DH) % CHUNKS == 0 else 1
    width = feat // chunks
    any_spec = pl.BlockSpec(memory_space=pl.ANY)
    vmem_spec = pl.BlockSpec(memory_space=pltpu.VMEM)
    dma = pltpu.SemaphoreType.DMA
    states, scores = pl.pallas_call(
        functools.partial(kernel, n_hist, n_tower),
        out_shape=(
            pltpu.VMEM((rows, feat), BF16),
            pltpu.VMEM((1, rows), F32),
        ),
        in_specs=[any_spec] * 11,
        out_specs=(vmem_spec, vmem_spec),
        scratch_shapes=[
            pltpu.VMEM((n_hist, chunks, rows, width), BF16),
            pltpu.VMEM((n_hist, 1, rows), jnp.int32),
            pltpu.VMEM(hist_keys.shape, BF16),
            pltpu.VMEM(hist_values.shape, BF16),
            pltpu.VMEM(time_bucket.shape, jnp.int32),
            pltpu.VMEM((1,) + hist_len.shape, jnp.int32),
            pltpu.VMEM((2 * n_tower, rows, feat), BF16),
            pltpu.VMEM(time_bias.shape[::-1], F32),
            pltpu.VMEM((2, feat, hidden), BF16),
            pltpu.VMEM((1, hidden), F32),
            pltpu.VMEM((1, hidden), F32),
            pltpu.VMEM((chunks, rows, width), F32),
            pltpu.VMEM((n_hist, chunks, rows, width), BF16),
            pltpu.VMEM((n_hist, chunks, rows, width), BF16),
            pltpu.VMEM((2 * n_tower, chunks, rows, width), BF16),
            pltpu.VMEM((n_tower, 1, rows), F32),
            pltpu.VMEM((2 * n_tower, 1, rows), F32),
            dma((10,)),
            dma,
            pltpu.SemaphoreType.REGULAR((n_hist,)),
            pltpu.SemaphoreType.REGULAR,
            dma,
            dma((n_hist, chunks)),
            dma,
            dma((n_hist,)),
            dma,
            dma((n_hist, chunks)),
            dma((1,)),
            dma((1,)),
            dma,
            dma((2 * n_tower,)),
            dma,
            dma((2 * n_tower,)),
            dma,
            dma((2 * n_tower,)),
        ],
        compiler_params=pltpu.CompilerParams(collective_id=0, has_side_effects=True),
    )(
        queries,
        hist_keys,
        hist_values,
        cand_user.reshape(1, rows),
        time_bucket,
        hist_len.reshape(1, -1),
        cand_gate,
        time_bias.T,
        tower_in,
        tower_bias.reshape(1, -1),
        tower_out.reshape(1, -1),
    )
    states, scores = pl.pallas_call(
        hand_over,
        out_shape=(
            jax.ShapeDtypeStruct((rows, feat), BF16),
            jax.ShapeDtypeStruct((1, rows), F32),
        ),
        in_specs=[vmem_spec, vmem_spec],
        out_specs=(any_spec, any_spec),
        scratch_shapes=[dma((2,))],
    )(
        pltpu.with_memory_space_constraint(states, pltpu.VMEM),
        pltpu.with_memory_space_constraint(scores, pltpu.VMEM),
    )
    return states, scores.reshape(rows)


def solution(mesh):
    return jax.shard_map(
        functools.partial(local, n_hist=mesh.shape["hist"], n_tower=mesh.shape["tower"]),
        mesh=mesh,
        in_specs=(
            P(("groups", "hist", "tower"), "head"),
            P("groups", "hist", "head"),
            P("groups", "hist", "head"),
            P(("groups", "hist", "tower")),
            P("groups", "hist"),
            P("groups"),
            P(("groups", "hist", "tower"), "head"),
            P(None, "head"),
            P("head", "tower"),
            P("tower"),
            P("tower"),
        ),
        out_specs=(P(("groups", "hist", "tower"), "head"), P(("groups", "hist", "tower"))),
        check_vma=False,
    )
```

```python
import functools

import jax
import jax.numpy as jnp
from jax import lax
from jax.experimental import pallas as pl
from jax.experimental.pallas import tpu as pltpu
from jax.sharding import PartitionSpec as P

DH = 128
CHUNKS = 2
MESH = pl.DeviceIdType.MESH
F32 = jnp.float32
BF16 = jnp.bfloat16


def partner_of(me, step, count):
    if count & (count - 1):
        return lax.rem(me + step, count)
    other, bit = 0, 1
    while bit < count:
        mine = lax.rem(me // bit, 2)
        other = other + (1 - mine if step & bit else mine) * bit
        bit *= 2
    return other


def source_of(me, step, count):
    if count & (count - 1):
        return lax.rem(me + count - step, count)
    return partner_of(me, step, count)


def relayed(block, at, count, core):
    gap, from_end = abs(block - at), block in (0, count - 1)
    return gap == 2 and not from_end or core == 1 and gap == 3 and from_end


def handed_on(block, at, count, core):
    there = at + (1 if at > block else -1)
    return there if 0 <= there < count and relayed(block, there, count, core) else None


def order_of(at, count, core):
    def key(block):
        hops = at - block if block < at else at + 0.6 * (block - at)
        passed = handed_on(block, at, count, core) is not None
        return not passed, relayed(block, at, count, core), hops

    return sorted((b for b in range(count) if b != at), key=key)


def pick(me, values):
    if all(v == values[0] for v in values):
        return values[0]
    chosen = jnp.int32(values[0])
    for i, v in enumerate(values[1:], 1):
        chosen = jnp.where(me == i, jnp.int32(v), chosen)
    return chosen


def when(condition):
    if isinstance(condition, bool):
        return (lambda body: body()) if condition else (lambda body: None)
    return pl.when(condition)


def kernel(
    n_hist,
    n_tower,
    q_hbm,
    k_hbm,
    v_hbm,
    user_hbm,
    bucket_hbm,
    len_hbm,
    gate_hbm,
    tbias_hbm,
    w_hbm,
    b_hbm,
    o_hbm,
    states_out,
    scores_out,
    q_all,
    u_all,
    k_buf,
    v_buf,
    bucket,
    len_ref,
    gate,
    tbias,
    w_buf,
    b_buf,
    o_buf,
    own_share,
    share_out,
    share_in,
    att_buf,
    score_send,
    score_in,
    load_sem,
    q_load,
    above,
    peers,
    q_send,
    q_recv,
    u_send,
    u_recv,
    share_send,
    share_recv,
    w_send,
    w_recv,
    gate_send,
    gate_recv,
    att_send,
    att_recv,
    score_send_sem,
    score_recv,
):
    z = lax.axis_index("hist")
    x = lax.axis_index("tower")
    c = lax.axis_index("head")
    mate = 1 - c
    rows, feat = q_hbm.shape
    users, per_user, _ = k_hbm.shape
    hidden = b_buf.shape[1]
    total_feat = 2 * feat
    chunks = q_all.shape[1]
    width = feat // chunks

    tower_peers = [(t, h) for t in range(n_tower) for h in range(2) if t or h]

    def tower_id(t, h):
        return {"tower": partner_of(x, t, n_tower), "head": mate if h else c}

    def rank_of(tower, head):
        return 2 * tower + 1 - head

    rank = rank_of(x, c)
    peer_ranks = [
        (t, h, rank_of(partner_of(x, t, n_tower), mate if h else c)) for t, h in tower_peers
    ]
    barrier = pltpu.get_barrier_semaphore()
    for distance in range(1, n_hist):

        @pl.when(z + distance < n_hist)
        def _(distance=distance):
            pl.semaphore_signal(
                barrier, inc=1, device_id={"hist": z + distance}, device_id_type=MESH
            )

    for t, h, other_rank in peer_ranks:

        @pl.when(other_rank > rank)
        def _(t=t, h=h):
            pl.semaphore_signal(barrier, inc=1, device_id=tower_id(t, h), device_id_type=MESH)

    mine_cols = pl.ds(pl.multiple_of(c * hidden, 128), hidden)
    mate_cols = pl.ds(pl.multiple_of(mate * hidden, 128), hidden)
    q_loads = [
        pltpu.make_async_copy(q_hbm.at[:, i * width : (i + 1) * width], q_all.at[z, i], q_load)
        for i in range(chunks)
    ]
    loads = [
        pltpu.make_async_copy(src, dst, load_sem.at[i])
        for i, (src, dst) in enumerate(
            [
                (user_hbm, u_all.at[z]),
                (bucket_hbm, bucket),
                (tbias_hbm, tbias),
                (len_hbm, len_ref),
                (k_hbm, k_buf),
                (v_hbm, v_buf),
                (gate_hbm, gate.at[2 * x + c]),
                (b_hbm.at[:, mine_cols], b_buf),
                (o_hbm.at[:, mine_cols], o_buf),
                (w_hbm.at[:, mine_cols], w_buf.at[c]),
            ]
        )
    ]
    user_load, bucket_load, tbias_load, len_load, k_load, v_load, *late_loads = loads
    for load in q_loads + loads[:6]:
        load.start()

    awaited = rank + z

    @pl.when(awaited > 0)
    def _():
        pl.semaphore_wait(barrier, awaited)

    for distance in range(1, n_hist):

        @pl.when(z >= distance)
        def _(distance=distance):
            pl.semaphore_signal(
                above.at[z], inc=1, device_id={"hist": z - distance}, device_id_type=MESH
            )

    for t, h, other_rank in peer_ranks:

        @pl.when(other_rank < rank)
        def _(t=t, h=h):
            pl.semaphore_signal(peers, inc=1, device_id=tower_id(t, h), device_id_type=MESH)

    def remote(src, dst, send, recv, device_id):
        return pltpu.make_async_remote_copy(
            src_ref=src,
            dst_ref=dst,
            send_sem=send,
            recv_sem=recv,
            device_id=device_id,
            device_id_type=MESH,
        )

    def query_copy(there, chunk):
        return remote(
            q_all.at[z, chunk],
            q_all.at[z, chunk],
            q_send,
            q_recv.at[z, chunk],
            {"hist": there},
        )

    def user_copy(there):
        return remote(u_all.at[z], u_all.at[z], u_send, u_recv.at[z], {"hist": there})

    def send_queries(there):
        user_copy(there).start()
        for chunk in range(chunks):
            query_copy(there, chunk).start()

    places = [(at, core) for at in range(n_hist) for core in range(2)]
    place = 2 * z + c

    def flag(values):
        chosen = pick(place, [int(v) for v in values])
        return bool(chosen) if isinstance(chosen, int) else chosen == 1

    def goes_direct(distance, sign):
        return flag(
            [
                not relayed(at, at + sign * distance, n_hist, core)
                if 0 <= at + sign * distance < n_hist
                else False
                for at, core in places
            ]
        )

    def send_down(distance):
        @pl.when(z >= distance)
        def _():
            when(goes_direct(distance, -1))(lambda: send_queries(z - distance))

    def send_up(distance, condition):
        @pl.when(condition)
        def _():
            pl.semaphore_wait(above.at[z + distance], 1)
            when(goes_direct(distance, 1))(lambda: send_queries(z + distance))

    user_load.wait()
    pltpu.make_async_copy(q_all.at[z], q_all.at[z], q_load).wait()
    for distance in range(n_hist - 1, 0, -1):
        send_down(distance)

    send_up(1, z < n_hist - 2)

    bucket_load.wait()
    tbias_load.wait()
    len_load.wait()
    heads, bucket_count = tbias.shape
    half_scale = 0.5 * DH ** (-0.5)
    tb = tbias[...] * 0.5
    bias_rows, owner_rows = [], []
    for u in range(users):
        onehot = jnp.where(
            lax.broadcasted_iota(jnp.int32, (bucket_count, per_user), 0) == bucket[u : u + 1, :],
            1.0,
            0.0,
        ).astype(F32)
        bias_rows.append(
            lax.dot_general(
                tb,
                onehot,
                (((1,), (0,)), ((), ())),
                precision=lax.Precision.HIGHEST,
                preferred_element_type=F32,
            )
        )
        position = z * per_user + lax.broadcasted_iota(jnp.int32, (1, per_user), 1)
        owner_rows.append(jnp.where(position < len_ref[:, u : u + 1], u, -1))
    bias = jnp.concatenate(bias_rows, axis=1)
    owner = jnp.concatenate(owner_rows, axis=1)
    events = users * per_user
    k_load.wait()
    v_load.wait()

    def live_of(index):
        user_col = jnp.broadcast_to(u_all[index], (128, rows)).T[:, :1]
        return jnp.where(user_col == owner, 1.0, 0.0).astype(F32)

    def scored(query, head):
        cols = slice(head * DH, (head + 1) * DH)
        return lax.dot_general(
            query,
            k_buf[:, :, cols].reshape(events, DH),
            (((1,), (1,)), ((), ())),
            preferred_element_type=F32,
        )

    def weighed(s, live, head):
        half = s * half_scale + bias[head : head + 1, :]
        return ((half + half * jnp.tanh(half)) * live).astype(BF16)

    def gathered(weight, head):
        cols = slice(head * DH, (head + 1) * DH)
        return jnp.dot(
            weight, v_buf[:, :, cols].reshape(events, DH), preferred_element_type=F32
        )

    per_chunk = heads // chunks

    def share_of(block, live, chunk):
        mine = [chunk * per_chunk + i for i in range(per_chunk)]
        s = [scored(q_all[block, chunk, :, i * DH : (i + 1) * DH], head) for i, head in enumerate(mine)]
        weights = [weighed(s[i], live, head) for i, head in enumerate(mine)]
        parts = [gathered(weights[i], head) for i, head in enumerate(mine)]
        return jnp.concatenate(parts, axis=1) if per_chunk > 1 else parts[0]

    own_live = live_of(z)
    for chunk in range(chunks):
        own_share[chunk] = share_of(z, own_live, chunk)

    for load in late_loads:
        load.start()

    send_up(1, z == n_hist - 2)
    for distance in range(2, n_hist):
        send_up(distance, z + distance < n_hist)


    @pl.when(rank < 2 * n_tower - 1)
    def _():
        pl.semaphore_wait(peers, 2 * n_tower - 1 - rank)
    w_copy = remote(
        w_hbm.at[:, mate_cols], w_buf.at[c], w_send.at[0], w_recv.at[0], {"head": mate}
    )
    w_copy.start()
    for i, (t, h) in enumerate(tower_peers):
        copy = remote(
            gate_hbm, gate.at[2 * x + c], gate_send, gate_recv.at[2 * x + c], tower_id(t, h)
        )
        copy.start()

    def user_arrives(block):
        remote(
            u_all.at[block], u_all.at[block], u_send, u_recv.at[block], {"hist": block}
        ).wait_recv()

    def query_arrives(block, chunk):
        remote(
            q_all.at[block, chunk],
            q_all.at[block, chunk],
            q_send,
            q_recv.at[block, chunk],
            {"hist": block},
        ).wait_recv()

    def pass_copy(step, block, there, chunk):
        return remote(
            q_all.at[block, chunk],
            q_all.at[block, chunk],
            q_send,
            q_recv.at[block, chunk],
            {"hist": there},
        )

    def pass_user(step, block, there):
        return remote(
            u_all.at[block],
            u_all.at[block],
            u_send,
            u_recv.at[block],
            {"hist": there},
        )

    def share_copy(step, chunk):
        return remote(
            share_out.at[step, chunk],
            share_in.at[z, chunk],
            share_send,
            share_recv.at[z, chunk],
            {"hist": steps[step][0]},
        )

    orders = [order_of(at, n_hist, core) for at, core in places]
    steps = []
    for step in range(n_hist - 1):
        blocks = [order[step] for order in orders]
        targets = [handed_on(b, at, n_hist, core) for b, (at, core) in zip(blocks, places)]
        steps.append(
            (
                pick(place, blocks),
                flag([there is not None for there in targets]),
                pick(place, [there or 0 for there in targets]),
            )
        )

    for step, (block, passing, there) in enumerate(steps):
        user_arrives(block)

        @when(passing)
        def _():
            pass_user(step, block, there).start()

        live = live_of(block)
        holding = not passing if isinstance(passing, bool) else jnp.logical_not(passing)

        @when(passing)
        def _():
            for chunk in range(chunks):
                query_arrives(block, chunk)
                pass_copy(step, block, there, chunk).start()

        for chunk in range(chunks):
            @when(holding)
            def _():
                query_arrives(block, chunk)

            share_out[step, chunk] = share_of(block, live, chunk).astype(BF16)
            share_copy(step, chunk).start()

    sources = [block for block, _, _ in steps]

    def att_copy(tower, head, chunk, device_id):
        return remote(
            att_buf.at[2 * tower + head, chunk],
            att_buf.at[2 * tower + head, chunk],
            att_send,
            att_recv.at[2 * tower + head],
            device_id,
        )

    own = []
    for chunk in range(chunks):
        for src in sources:
            remote(
                share_out.at[0, chunk],
                share_in.at[src, chunk],
                share_send,
                share_recv.at[src, chunk],
                {"hist": src},
            ).wait_recv()
        part = own_share[chunk]
        for src in sources:
            part = part + share_in[src, chunk].astype(F32)
        own.append(part)
        att_buf[2 * x + c, chunk] = part.astype(BF16)
        for t in range(1, n_tower):
            for head in range(2):
                att_copy(x, c, chunk, {"tower": partner_of(x, t, n_tower), "head": head}).start()
        att_copy(x, c, chunk, {"head": mate}).start()

    def half_arrives(tower, head):
        remote(
            gate_hbm, gate.at[2 * tower + head], gate_send, gate_recv.at[2 * tower + head], {"head": mate}
        ).wait_recv()
        remote(
            att_buf.at[2 * tower + head],
            att_buf.at[2 * tower + head],
            att_send,
            att_recv.at[2 * tower + head],
            {"head": mate},
        ).wait_recv()

    def half_of(tower, head):
        return [att_buf[2 * tower + head, chunk].astype(F32) for chunk in range(chunks)]

    def normalised(pieces, gates):
        every = [p for half in pieces for p in half]
        row_sum = sum(jnp.sum(p, axis=1, keepdims=True) for p in every)
        row_squares = sum(jnp.sum(p * p, axis=1, keepdims=True) for p in every)
        row_mean = row_sum / total_feat
        row_var = row_squares / total_feat - row_mean * row_mean
        scale = lax.rsqrt(row_var + 1e-05)
        return [
            ((jnp.concatenate(half, axis=1) - row_mean) * scale * g.astype(F32)).astype(BF16)
            for half, g in zip(pieces, gates)
        ]

    for load in late_loads:
        load.wait()
    remote(
        w_hbm.at[:, mate_cols], w_buf.at[mate], w_send.at[0], w_recv.at[0], {"head": mate}
    ).wait_recv()

    def scores_of(first, first_w, second, second_w):
        pre = jnp.dot(first, w_buf[first_w], preferred_element_type=F32)
        pre = pre + jnp.dot(second, w_buf[second_w], preferred_element_type=F32)
        half = (pre + b_buf[...]) * 0.5
        part = (half + half * jnp.tanh(half)) * o_buf[...]
        acc = part[:, 0:128]
        for i in range(1, hidden // 128):
            acc = acc + part[:, i * 128 : (i + 1) * 128]
        return jnp.sum(acc.T, axis=0, keepdims=True)

    half_arrives(x, mate)
    mine, theirs = normalised([own, half_of(x, mate)], [gate[2 * x + c], gate[2 * x + mate]])
    states_out[...] = mine
    own_scores = scores_of(mine, c, theirs, mate)
    score_in[2 * x + c] = own_scores
    copy = remote(
        score_in.at[2 * x + c], score_in.at[2 * x + c], score_send_sem, score_recv.at[2 * x + c], {"head": mate}
    )
    copy.start()
    for t in range(1, n_tower):
        other = source_of(x, t, n_tower)
        half_arrives(other, c)
        half_arrives(other, mate)
        first, second = normalised(
            [half_of(other, 0), half_of(other, 1)], [gate[2 * other], gate[2 * other + 1]]
        )
        score_send[t] = scores_of(first, 0, second, 1)
        for h in range(2):
            copy = remote(
                score_send.at[t],
                score_in.at[2 * x + c],
                score_send_sem,
                score_recv.at[2 * x + c],
                {"tower": other, "head": h},
            )
            copy.start()

    for t, h in tower_peers:
        tower, head = partner_of(x, t, n_tower), mate if h else c
        remote(
            score_in.at[2 * tower + head],
            score_in.at[2 * tower + head],
            score_send_sem,
            score_recv.at[2 * tower + head],
            {"head": mate},
        ).wait_recv()
    total = score_in[0] + score_in[1]
    for t in range(1, n_tower):
        total = total + (score_in[2 * t] + score_in[2 * t + 1])
    scores_out[...] = total
    w_copy.wait_send()
    sent = [
        sum(
            (not relayed(at, b, n_hist, core)) + (handed_on(b, at, n_hist, core) is not None)
            for b in range(n_hist)
            if b != at
        )
        for at, core in places
    ]
    for count in sorted(set(sent)):

        @when(flag([n == count for n in sent]))
        def _(count=count):
            for ref, send, recv in (
                (q_all.at[0:count], q_send, q_recv.at[0, 0]),
                (u_all.at[0:count], u_send, u_recv.at[0]),
            ):
                remote(ref, ref, send, recv, {"head": mate}).wait_send()

    others, peer_count = slice(0, n_hist - 1), slice(0, 2 * n_tower - 1)
    for ref, send, recv in (
        (share_out.at[others], share_send, share_recv.at[0, 0]),
        (gate.at[peer_count], gate_send, gate_recv.at[0]),
        (att_buf.at[peer_count], att_send, att_recv.at[0]),
        (score_in.at[peer_count], score_send_sem, score_recv.at[0]),
    ):
        remote(ref, ref, send, recv, {"head": mate}).wait_send()


def hand_over(states_in, scores_in, states_out, scores_out, sems):
    copies = [
        pltpu.make_async_copy(states_in, states_out, sems.at[0]),
        pltpu.make_async_copy(scores_in, scores_out, sems.at[1]),
    ]
    for copy in copies:
        copy.start()
    for copy in copies:
        copy.wait()


def local(
    queries,
    hist_keys,
    hist_values,
    cand_user,
    time_bucket,
    hist_len,
    cand_gate,
    time_bias,
    tower_in,
    tower_bias,
    tower_out,
    *,
    n_hist,
    n_tower,
):
    rows, feat = queries.shape
    hidden = tower_in.shape[1] // 2
    chunks = CHUNKS if (feat // DH) % CHUNKS == 0 else 1
    width = feat // chunks
    any_spec = pl.BlockSpec(memory_space=pl.ANY)
    vmem_spec = pl.BlockSpec(memory_space=pltpu.VMEM)
    dma = pltpu.SemaphoreType.DMA
    states, scores = pl.pallas_call(
        functools.partial(kernel, n_hist, n_tower),
        out_shape=(
            pltpu.VMEM((rows, feat), BF16),
            pltpu.VMEM((1, rows), F32),
        ),
        in_specs=[any_spec] * 11,
        out_specs=(vmem_spec, vmem_spec),
        scratch_shapes=[
            pltpu.VMEM((n_hist, chunks, rows, width), BF16),
            pltpu.VMEM((n_hist, 1, rows), jnp.int32),
            pltpu.VMEM(hist_keys.shape, BF16),
            pltpu.VMEM(hist_values.shape, BF16),
            pltpu.VMEM(time_bucket.shape, jnp.int32),
            pltpu.VMEM((1,) + hist_len.shape, jnp.int32),
            pltpu.VMEM((2 * n_tower, rows, feat), BF16),
            pltpu.VMEM(time_bias.shape[::-1], F32),
            pltpu.VMEM((2, feat, hidden), BF16),
            pltpu.VMEM((1, hidden), F32),
            pltpu.VMEM((1, hidden), F32),
            pltpu.VMEM((chunks, rows, width), F32),
            pltpu.VMEM((n_hist, chunks, rows, width), BF16),
            pltpu.VMEM((n_hist, chunks, rows, width), BF16),
            pltpu.VMEM((2 * n_tower, chunks, rows, width), BF16),
            pltpu.VMEM((n_tower, 1, rows), F32),
            pltpu.VMEM((2 * n_tower, 1, rows), F32),
            dma((10,)),
            dma,
            pltpu.SemaphoreType.REGULAR((n_hist,)),
            pltpu.SemaphoreType.REGULAR,
            dma,
            dma((n_hist, chunks)),
            dma,
            dma((n_hist,)),
            dma,
            dma((n_hist, chunks)),
            dma((1,)),
            dma((1,)),
            dma,
            dma((2 * n_tower,)),
            dma,
            dma((2 * n_tower,)),
            dma,
            dma((2 * n_tower,)),
        ],
        compiler_params=pltpu.CompilerParams(collective_id=0, has_side_effects=True),
    )(
        queries,
        hist_keys,
        hist_values,
        cand_user.reshape(1, rows),
        time_bucket,
        hist_len.reshape(1, -1),
        cand_gate,
        time_bias.T,
        tower_in,
        tower_bias.reshape(1, -1),
        tower_out.reshape(1, -1),
    )
    states, scores = pl.pallas_call(
        hand_over,
        out_shape=(
            jax.ShapeDtypeStruct((rows, feat), BF16),
            jax.ShapeDtypeStruct((1, rows), F32),
        ),
        in_specs=[vmem_spec, vmem_spec],
        out_specs=(any_spec, any_spec),
        scratch_shapes=[dma((2,))],
    )(
        pltpu.with_memory_space_constraint(states, pltpu.VMEM),
        pltpu.with_memory_space_constraint(scores, pltpu.VMEM),
    )
    return states, scores.reshape(rows)


def solution(mesh):
    return jax.shard_map(
        functools.partial(local, n_hist=mesh.shape["hist"], n_tower=mesh.shape["tower"]),
        mesh=mesh,
        in_specs=(
            P(("groups", "hist", "tower"), "head"),
            P("groups", "hist", "head"),
            P("groups", "hist", "head"),
            P(("groups", "hist", "tower")),
            P("groups", "hist"),
            P("groups"),
            P(("groups", "hist", "tower"), "head"),
            P(None, "head"),
            P("head", "tower"),
            P("tower"),
            P("tower"),
        ),
        out_specs=(P(("groups", "hist", "tower"), "head"), P(("groups", "hist", "tower"))),
        check_vma=False,
    )
```

```python
import functools

import jax
import jax.numpy as jnp
from jax import lax
from jax.experimental import pallas as pl
from jax.experimental.pallas import tpu as pltpu
from jax.sharding import PartitionSpec as P

DH = 128
CHUNKS = 2
MESH = pl.DeviceIdType.MESH
F32 = jnp.float32
BF16 = jnp.bfloat16


def partner_of(me, step, count):
    if count & (count - 1):
        return lax.rem(me + step, count)
    other, bit = 0, 1
    while bit < count:
        mine = lax.rem(me // bit, 2)
        other = other + (1 - mine if step & bit else mine) * bit
        bit *= 2
    return other


def source_of(me, step, count):
    if count & (count - 1):
        return lax.rem(me + count - step, count)
    return partner_of(me, step, count)


def relayed(block, at, count, core):
    gap, from_end = abs(block - at), block in (0, count - 1)
    return gap == 2 and not from_end or core == 1 and gap == 3 and from_end


def handed_on(block, at, count, core):
    there = at + (1 if at > block else -1)
    return there if 0 <= there < count and relayed(block, there, count, core) else None


def order_of(at, count, core):
    def key(block):
        passed = handed_on(block, at, count, core) is not None
        if 2 * at < count:
            return core == 0 and not passed, block
        hops = at - block if block < at else at + 0.6 * (block - at)
        return not passed, relayed(block, at, count, core), hops

    return sorted((b for b in range(count) if b != at), key=key)


def pick(me, values):
    if all(v == values[0] for v in values):
        return values[0]
    chosen = jnp.int32(values[0])
    for i, v in enumerate(values[1:], 1):
        chosen = jnp.where(me == i, jnp.int32(v), chosen)
    return chosen


def when(condition):
    if isinstance(condition, bool):
        return (lambda body: body()) if condition else (lambda body: None)
    return pl.when(condition)


def kernel(
    n_hist,
    n_tower,
    q_hbm,
    k_hbm,
    v_hbm,
    user_hbm,
    bucket_hbm,
    len_hbm,
    gate_hbm,
    tbias_hbm,
    w_hbm,
    b_hbm,
    o_hbm,
    states_out,
    scores_out,
    q_all,
    u_all,
    k_buf,
    v_buf,
    bucket,
    len_ref,
    gate,
    tbias,
    w_buf,
    b_buf,
    o_buf,
    own_share,
    share_out,
    share_in,
    att_buf,
    score_send,
    score_in,
    load_sem,
    q_load,
    above,
    peers,
    q_send,
    q_recv,
    u_send,
    u_recv,
    share_send,
    share_recv,
    w_send,
    w_recv,
    gate_send,
    gate_recv,
    att_send,
    att_recv,
    score_send_sem,
    score_recv,
):
    z = lax.axis_index("hist")
    x = lax.axis_index("tower")
    c = lax.axis_index("head")
    mate = 1 - c
    rows, feat = q_hbm.shape
    users, per_user, _ = k_hbm.shape
    hidden = b_buf.shape[1]
    total_feat = 2 * feat
    chunks = q_all.shape[1]
    width = feat // chunks

    tower_peers = [(t, h) for t in range(n_tower) for h in range(2) if t or h]

    def tower_id(t, h):
        return {"tower": partner_of(x, t, n_tower), "head": mate if h else c}

    def rank_of(tower, head):
        return 2 * tower + 1 - head

    rank = rank_of(x, c)
    peer_ranks = [
        (t, h, rank_of(partner_of(x, t, n_tower), mate if h else c)) for t, h in tower_peers
    ]
    barrier = pltpu.get_barrier_semaphore()
    for distance in range(1, n_hist):

        @pl.when(z + distance < n_hist)
        def _(distance=distance):
            pl.semaphore_signal(
                barrier, inc=1, device_id={"hist": z + distance}, device_id_type=MESH
            )

    for t, h, other_rank in peer_ranks:

        @pl.when(other_rank > rank)
        def _(t=t, h=h):
            pl.semaphore_signal(barrier, inc=1, device_id=tower_id(t, h), device_id_type=MESH)

    mine_cols = pl.ds(pl.multiple_of(c * hidden, 128), hidden)
    mate_cols = pl.ds(pl.multiple_of(mate * hidden, 128), hidden)
    q_loads = [
        pltpu.make_async_copy(q_hbm.at[:, i * width : (i + 1) * width], q_all.at[z, i], q_load)
        for i in range(chunks)
    ]
    loads = [
        pltpu.make_async_copy(src, dst, load_sem.at[i])
        for i, (src, dst) in enumerate(
            [
                (user_hbm, u_all.at[z]),
                (bucket_hbm, bucket),
                (tbias_hbm, tbias),
                (len_hbm, len_ref),
                (k_hbm, k_buf),
                (v_hbm, v_buf),
                (gate_hbm, gate.at[2 * x + c]),
                (b_hbm.at[:, mine_cols], b_buf),
                (o_hbm.at[:, mine_cols], o_buf),
                (w_hbm.at[:, mine_cols], w_buf.at[c]),
            ]
        )
    ]
    user_load, bucket_load, tbias_load, len_load, k_load, v_load, *late_loads = loads
    for load in q_loads + loads[:6]:
        load.start()

    awaited = rank + z

    @pl.when(awaited > 0)
    def _():
        pl.semaphore_wait(barrier, awaited)

    for distance in range(1, n_hist):

        @pl.when(z >= distance)
        def _(distance=distance):
            pl.semaphore_signal(
                above.at[z], inc=1, device_id={"hist": z - distance}, device_id_type=MESH
            )

    for t, h, other_rank in peer_ranks:

        @pl.when(other_rank < rank)
        def _(t=t, h=h):
            pl.semaphore_signal(peers, inc=1, device_id=tower_id(t, h), device_id_type=MESH)

    def remote(src, dst, send, recv, device_id):
        return pltpu.make_async_remote_copy(
            src_ref=src,
            dst_ref=dst,
            send_sem=send,
            recv_sem=recv,
            device_id=device_id,
            device_id_type=MESH,
        )

    def query_copy(there, chunk):
        return remote(
            q_all.at[z, chunk],
            q_all.at[z, chunk],
            q_send,
            q_recv.at[z, chunk],
            {"hist": there},
        )

    def user_copy(there):
        return remote(u_all.at[z], u_all.at[z], u_send, u_recv.at[z], {"hist": there})

    def send_queries(there):
        user_copy(there).start()
        for chunk in range(chunks):
            query_copy(there, chunk).start()

    places = [(at, core) for at in range(n_hist) for core in range(2)]
    place = 2 * z + c

    def flag(values):
        chosen = pick(place, [int(v) for v in values])
        return bool(chosen) if isinstance(chosen, int) else chosen == 1

    def goes_direct(distance, sign):
        return flag(
            [
                not relayed(at, at + sign * distance, n_hist, core)
                if 0 <= at + sign * distance < n_hist
                else False
                for at, core in places
            ]
        )

    def send_down(distance):
        @pl.when(z >= distance)
        def _():
            when(goes_direct(distance, -1))(lambda: send_queries(z - distance))

    def send_up(distance, condition):
        @pl.when(condition)
        def _():
            pl.semaphore_wait(above.at[z + distance], 1)
            when(goes_direct(distance, 1))(lambda: send_queries(z + distance))

    user_load.wait()
    pltpu.make_async_copy(q_all.at[z], q_all.at[z], q_load).wait()
    for distance in range(n_hist - 1, 0, -1):
        send_down(distance)

    send_up(1, z < n_hist - 2)

    bucket_load.wait()
    tbias_load.wait()
    len_load.wait()
    heads, bucket_count = tbias.shape
    half_scale = 0.5 * DH ** (-0.5)
    tb = tbias[...] * 0.5
    bias_rows, owner_rows = [], []
    for u in range(users):
        onehot = jnp.where(
            lax.broadcasted_iota(jnp.int32, (bucket_count, per_user), 0) == bucket[u : u + 1, :],
            1.0,
            0.0,
        ).astype(F32)
        bias_rows.append(
            lax.dot_general(
                tb,
                onehot,
                (((1,), (0,)), ((), ())),
                precision=lax.Precision.HIGHEST,
                preferred_element_type=F32,
            )
        )
        position = z * per_user + lax.broadcasted_iota(jnp.int32, (1, per_user), 1)
        owner_rows.append(jnp.where(position < len_ref[:, u : u + 1], u, -1))
    bias = jnp.concatenate(bias_rows, axis=1)
    owner = jnp.concatenate(owner_rows, axis=1)
    events = users * per_user
    k_load.wait()
    v_load.wait()

    def live_of(index):
        user_col = jnp.broadcast_to(u_all[index], (128, rows)).T[:, :1]
        return jnp.where(user_col == owner, 1.0, 0.0).astype(F32)

    def scored(query, head):
        cols = slice(head * DH, (head + 1) * DH)
        return lax.dot_general(
            query,
            k_buf[:, :, cols].reshape(events, DH),
            (((1,), (1,)), ((), ())),
            preferred_element_type=F32,
        )

    def weighed(s, live, head):
        half = s * half_scale + bias[head : head + 1, :]
        return ((half + half * jnp.tanh(half)) * live).astype(BF16)

    def gathered(weight, head):
        cols = slice(head * DH, (head + 1) * DH)
        return jnp.dot(
            weight, v_buf[:, :, cols].reshape(events, DH), preferred_element_type=F32
        )

    per_chunk = heads // chunks

    def share_of(block, live, chunk):
        mine = [chunk * per_chunk + i for i in range(per_chunk)]
        s = [scored(q_all[block, chunk, :, i * DH : (i + 1) * DH], head) for i, head in enumerate(mine)]
        weights = [weighed(s[i], live, head) for i, head in enumerate(mine)]
        parts = [gathered(weights[i], head) for i, head in enumerate(mine)]
        return jnp.concatenate(parts, axis=1) if per_chunk > 1 else parts[0]

    own_live = live_of(z)
    for chunk in range(chunks):
        own_share[chunk] = share_of(z, own_live, chunk)

    for load in late_loads:
        load.start()

    send_up(1, z == n_hist - 2)
    for distance in range(2, n_hist):
        send_up(distance, z + distance < n_hist)


    @pl.when(rank < 2 * n_tower - 1)
    def _():
        pl.semaphore_wait(peers, 2 * n_tower - 1 - rank)
    w_copy = remote(
        w_hbm.at[:, mate_cols], w_buf.at[c], w_send.at[0], w_recv.at[0], {"head": mate}
    )
    w_copy.start()
    for i, (t, h) in enumerate(tower_peers):
        copy = remote(
            gate_hbm, gate.at[2 * x + c], gate_send, gate_recv.at[2 * x + c], tower_id(t, h)
        )
        copy.start()

    def user_arrives(block):
        remote(
            u_all.at[block], u_all.at[block], u_send, u_recv.at[block], {"hist": block}
        ).wait_recv()

    def query_arrives(block, chunk):
        remote(
            q_all.at[block, chunk],
            q_all.at[block, chunk],
            q_send,
            q_recv.at[block, chunk],
            {"hist": block},
        ).wait_recv()

    def pass_copy(step, block, there, chunk):
        return remote(
            q_all.at[block, chunk],
            q_all.at[block, chunk],
            q_send,
            q_recv.at[block, chunk],
            {"hist": there},
        )

    def pass_user(step, block, there):
        return remote(
            u_all.at[block],
            u_all.at[block],
            u_send,
            u_recv.at[block],
            {"hist": there},
        )

    def share_copy(step, chunk):
        return remote(
            share_out.at[step, chunk],
            share_in.at[z, chunk],
            share_send,
            share_recv.at[z, chunk],
            {"hist": steps[step][0]},
        )

    orders = [order_of(at, n_hist, core) for at, core in places]
    steps = []
    for step in range(n_hist - 1):
        blocks = [order[step] for order in orders]
        targets = [handed_on(b, at, n_hist, core) for b, (at, core) in zip(blocks, places)]
        steps.append(
            (
                pick(place, blocks),
                flag([there is not None for there in targets]),
                pick(place, [there or 0 for there in targets]),
            )
        )

    for step, (block, passing, there) in enumerate(steps):
        user_arrives(block)

        @when(passing)
        def _():
            pass_user(step, block, there).start()

        live = live_of(block)
        holding = not passing if isinstance(passing, bool) else jnp.logical_not(passing)

        @when(passing)
        def _():
            for chunk in range(chunks):
                query_arrives(block, chunk)
                pass_copy(step, block, there, chunk).start()

        for chunk in range(chunks):
            @when(holding)
            def _():
                query_arrives(block, chunk)

            share_out[step, chunk] = share_of(block, live, chunk).astype(BF16)
            share_copy(step, chunk).start()

    sources = [block for block, _, _ in steps]

    def att_copy(tower, head, chunk, device_id):
        return remote(
            att_buf.at[2 * tower + head, chunk],
            att_buf.at[2 * tower + head, chunk],
            att_send,
            att_recv.at[2 * tower + head],
            device_id,
        )

    own = []
    for chunk in range(chunks):
        for src in sources:
            remote(
                share_out.at[0, chunk],
                share_in.at[src, chunk],
                share_send,
                share_recv.at[src, chunk],
                {"hist": src},
            ).wait_recv()
        part = own_share[chunk]
        for src in sources:
            part = part + share_in[src, chunk].astype(F32)
        own.append(part)
        att_buf[2 * x + c, chunk] = part.astype(BF16)
        for t in range(1, n_tower):
            for head in range(2):
                att_copy(x, c, chunk, {"tower": partner_of(x, t, n_tower), "head": head}).start()
        att_copy(x, c, chunk, {"head": mate}).start()

    def half_arrives(tower, head):
        remote(
            gate_hbm, gate.at[2 * tower + head], gate_send, gate_recv.at[2 * tower + head], {"head": mate}
        ).wait_recv()
        remote(
            att_buf.at[2 * tower + head],
            att_buf.at[2 * tower + head],
            att_send,
            att_recv.at[2 * tower + head],
            {"head": mate},
        ).wait_recv()

    def half_of(tower, head):
        return [att_buf[2 * tower + head, chunk].astype(F32) for chunk in range(chunks)]

    def normalised(pieces, gates):
        every = [p for half in pieces for p in half]
        row_sum = sum(jnp.sum(p, axis=1, keepdims=True) for p in every)
        row_squares = sum(jnp.sum(p * p, axis=1, keepdims=True) for p in every)
        row_mean = row_sum / total_feat
        row_var = row_squares / total_feat - row_mean * row_mean
        scale = lax.rsqrt(row_var + 1e-05)
        return [
            ((jnp.concatenate(half, axis=1) - row_mean) * scale * g.astype(F32)).astype(BF16)
            for half, g in zip(pieces, gates)
        ]

    for load in late_loads:
        load.wait()
    remote(
        w_hbm.at[:, mate_cols], w_buf.at[mate], w_send.at[0], w_recv.at[0], {"head": mate}
    ).wait_recv()

    def scores_of(first, first_w, second, second_w):
        pre = jnp.dot(first, w_buf[first_w], preferred_element_type=F32)
        pre = pre + jnp.dot(second, w_buf[second_w], preferred_element_type=F32)
        half = (pre + b_buf[...]) * 0.5
        part = (half + half * jnp.tanh(half)) * o_buf[...]
        acc = part[:, 0:128]
        for i in range(1, hidden // 128):
            acc = acc + part[:, i * 128 : (i + 1) * 128]
        return jnp.sum(acc.T, axis=0, keepdims=True)

    half_arrives(x, mate)
    mine, theirs = normalised([own, half_of(x, mate)], [gate[2 * x + c], gate[2 * x + mate]])
    states_out[...] = mine
    own_scores = scores_of(mine, c, theirs, mate)
    score_in[2 * x + c] = own_scores
    copy = remote(
        score_in.at[2 * x + c], score_in.at[2 * x + c], score_send_sem, score_recv.at[2 * x + c], {"head": mate}
    )
    copy.start()
    for t in range(1, n_tower):
        other = source_of(x, t, n_tower)
        half_arrives(other, c)
        half_arrives(other, mate)
        first, second = normalised(
            [half_of(other, 0), half_of(other, 1)], [gate[2 * other], gate[2 * other + 1]]
        )
        score_send[t] = scores_of(first, 0, second, 1)
        for h in range(2):
            copy = remote(
                score_send.at[t],
                score_in.at[2 * x + c],
                score_send_sem,
                score_recv.at[2 * x + c],
                {"tower": other, "head": h},
            )
            copy.start()

    for t, h in tower_peers:
        tower, head = partner_of(x, t, n_tower), mate if h else c
        remote(
            score_in.at[2 * tower + head],
            score_in.at[2 * tower + head],
            score_send_sem,
            score_recv.at[2 * tower + head],
            {"head": mate},
        ).wait_recv()
    total = score_in[0] + score_in[1]
    for t in range(1, n_tower):
        total = total + (score_in[2 * t] + score_in[2 * t + 1])
    scores_out[...] = total
    w_copy.wait_send()
    sent = [
        sum(
            (not relayed(at, b, n_hist, core)) + (handed_on(b, at, n_hist, core) is not None)
            for b in range(n_hist)
            if b != at
        )
        for at, core in places
    ]
    for count in sorted(set(sent)):

        @when(flag([n == count for n in sent]))
        def _(count=count):
            for ref, send, recv in (
                (q_all.at[0:count], q_send, q_recv.at[0, 0]),
                (u_all.at[0:count], u_send, u_recv.at[0]),
            ):
                remote(ref, ref, send, recv, {"head": mate}).wait_send()

    others, peer_count = slice(0, n_hist - 1), slice(0, 2 * n_tower - 1)
    for ref, send, recv in (
        (share_out.at[others], share_send, share_recv.at[0, 0]),
        (gate.at[peer_count], gate_send, gate_recv.at[0]),
        (att_buf.at[peer_count], att_send, att_recv.at[0]),
        (score_in.at[peer_count], score_send_sem, score_recv.at[0]),
    ):
        remote(ref, ref, send, recv, {"head": mate}).wait_send()


def hand_over(states_in, scores_in, states_out, scores_out, sems):
    copies = [
        pltpu.make_async_copy(states_in, states_out, sems.at[0]),
        pltpu.make_async_copy(scores_in, scores_out, sems.at[1]),
    ]
    for copy in copies:
        copy.start()
    for copy in copies:
        copy.wait()


def local(
    queries,
    hist_keys,
    hist_values,
    cand_user,
    time_bucket,
    hist_len,
    cand_gate,
    time_bias,
    tower_in,
    tower_bias,
    tower_out,
    *,
    n_hist,
    n_tower,
):
    rows, feat = queries.shape
    hidden = tower_in.shape[1] // 2
    chunks = CHUNKS if (feat // DH) % CHUNKS == 0 else 1
    width = feat // chunks
    any_spec = pl.BlockSpec(memory_space=pl.ANY)
    vmem_spec = pl.BlockSpec(memory_space=pltpu.VMEM)
    dma = pltpu.SemaphoreType.DMA
    states, scores = pl.pallas_call(
        functools.partial(kernel, n_hist, n_tower),
        out_shape=(
            pltpu.VMEM((rows, feat), BF16),
            pltpu.VMEM((1, rows), F32),
        ),
        in_specs=[any_spec] * 11,
        out_specs=(vmem_spec, vmem_spec),
        scratch_shapes=[
            pltpu.VMEM((n_hist, chunks, rows, width), BF16),
            pltpu.VMEM((n_hist, 1, rows), jnp.int32),
            pltpu.VMEM(hist_keys.shape, BF16),
            pltpu.VMEM(hist_values.shape, BF16),
            pltpu.VMEM(time_bucket.shape, jnp.int32),
            pltpu.VMEM((1,) + hist_len.shape, jnp.int32),
            pltpu.VMEM((2 * n_tower, rows, feat), BF16),
            pltpu.VMEM(time_bias.shape[::-1], F32),
            pltpu.VMEM((2, feat, hidden), BF16),
            pltpu.VMEM((1, hidden), F32),
            pltpu.VMEM((1, hidden), F32),
            pltpu.VMEM((chunks, rows, width), F32),
            pltpu.VMEM((n_hist, chunks, rows, width), BF16),
            pltpu.VMEM((n_hist, chunks, rows, width), BF16),
            pltpu.VMEM((2 * n_tower, chunks, rows, width), BF16),
            pltpu.VMEM((n_tower, 1, rows), F32),
            pltpu.VMEM((2 * n_tower, 1, rows), F32),
            dma((10,)),
            dma,
            pltpu.SemaphoreType.REGULAR((n_hist,)),
            pltpu.SemaphoreType.REGULAR,
            dma,
            dma((n_hist, chunks)),
            dma,
            dma((n_hist,)),
            dma,
            dma((n_hist, chunks)),
            dma((1,)),
            dma((1,)),
            dma,
            dma((2 * n_tower,)),
            dma,
            dma((2 * n_tower,)),
            dma,
            dma((2 * n_tower,)),
        ],
        compiler_params=pltpu.CompilerParams(collective_id=0, has_side_effects=True),
    )(
        queries,
        hist_keys,
        hist_values,
        cand_user.reshape(1, rows),
        time_bucket,
        hist_len.reshape(1, -1),
        cand_gate,
        time_bias.T,
        tower_in,
        tower_bias.reshape(1, -1),
        tower_out.reshape(1, -1),
    )
    states, scores = pl.pallas_call(
        hand_over,
        out_shape=(
            jax.ShapeDtypeStruct((rows, feat), BF16),
            jax.ShapeDtypeStruct((1, rows), F32),
        ),
        in_specs=[vmem_spec, vmem_spec],
        out_specs=(any_spec, any_spec),
        scratch_shapes=[dma((2,))],
    )(
        pltpu.with_memory_space_constraint(states, pltpu.VMEM),
        pltpu.with_memory_space_constraint(scores, pltpu.VMEM),
    )
    return states, scores.reshape(rows)


def solution(mesh):
    return jax.shard_map(
        functools.partial(local, n_hist=mesh.shape["hist"], n_tower=mesh.shape["tower"]),
        mesh=mesh,
        in_specs=(
            P(("groups", "hist", "tower"), "head"),
            P("groups", "hist", "head"),
            P("groups", "hist", "head"),
            P(("groups", "hist", "tower")),
            P("groups", "hist"),
            P("groups"),
            P(("groups", "hist", "tower"), "head"),
            P(None, "head"),
            P("head", "tower"),
            P("tower"),
            P("tower"),
        ),
        out_specs=(P(("groups", "hist", "tower"), "head"), P(("groups", "hist", "tower"))),
        check_vma=False,
    )
```

```python
import functools

import jax
import jax.numpy as jnp
from jax import lax
from jax.experimental import pallas as pl
from jax.experimental.pallas import tpu as pltpu
from jax.sharding import PartitionSpec as P

DH = 128
CHUNKS = 2
MESH = pl.DeviceIdType.MESH
F32 = jnp.float32
BF16 = jnp.bfloat16


def partner_of(me, step, count):
    if count & (count - 1):
        return lax.rem(me + step, count)
    other, bit = 0, 1
    while bit < count:
        mine = lax.rem(me // bit, 2)
        other = other + (1 - mine if step & bit else mine) * bit
        bit *= 2
    return other


def source_of(me, step, count):
    if count & (count - 1):
        return lax.rem(me + count - step, count)
    return partner_of(me, step, count)


def relayed(block, at, count, core):
    gap, from_end = abs(block - at), block in (0, count - 1)
    return gap == 2 and not from_end or core == 1 and gap == 3 and from_end


def handed_on(block, at, count, core):
    there = at + (1 if at > block else -1)
    return there if 0 <= there < count and relayed(block, there, count, core) else None


def order_of(at, count, core):
    def key(block):
        passed = handed_on(block, at, count, core) is not None
        if 2 * at < count:
            return core == 0 and not passed, block
        hops = at - block if block < at else at + 0.6 * (block - at)
        return not passed, relayed(block, at, count, core), hops

    return sorted((b for b in range(count) if b != at), key=key)


def pick(me, values):
    if all(v == values[0] for v in values):
        return values[0]
    chosen = jnp.int32(values[0])
    for i, v in enumerate(values[1:], 1):
        chosen = jnp.where(me == i, jnp.int32(v), chosen)
    return chosen


def when(condition):
    if isinstance(condition, bool):
        return (lambda body: body()) if condition else (lambda body: None)
    return pl.when(condition)


def kernel(
    n_hist,
    n_tower,
    q_hbm,
    k_hbm,
    v_hbm,
    user_hbm,
    bucket_hbm,
    len_hbm,
    gate_hbm,
    tbias_hbm,
    w_hbm,
    b_hbm,
    o_hbm,
    states_out,
    scores_out,
    q_all,
    u_all,
    k_buf,
    v_buf,
    bucket,
    len_ref,
    gate,
    tbias,
    w_buf,
    b_buf,
    o_buf,
    own_share,
    share_out,
    share_in,
    att_buf,
    score_send,
    score_in,
    load_sem,
    q_load,
    above,
    peers,
    q_send,
    q_recv,
    u_send,
    u_recv,
    share_send,
    share_recv,
    w_send,
    w_recv,
    gate_send,
    gate_recv,
    att_send,
    att_recv,
    score_send_sem,
    score_recv,
):
    z = lax.axis_index("hist")
    x = lax.axis_index("tower")
    c = lax.axis_index("head")
    mate = 1 - c
    rows, feat = q_hbm.shape
    users, per_user, _ = k_hbm.shape
    hidden = b_buf.shape[1]
    total_feat = 2 * feat
    chunks = q_all.shape[1]
    width = feat // chunks

    tower_peers = [(t, h) for t in range(n_tower) for h in range(2) if t or h]

    def tower_id(t, h):
        return {"tower": partner_of(x, t, n_tower), "head": mate if h else c}

    def rank_of(tower, head):
        return 2 * tower + 1 - head

    rank = rank_of(x, c)
    peer_ranks = [
        (t, h, rank_of(partner_of(x, t, n_tower), mate if h else c)) for t, h in tower_peers
    ]
    barrier = pltpu.get_barrier_semaphore()
    for distance in range(1, n_hist):

        @pl.when(z + distance < n_hist)
        def _(distance=distance):
            pl.semaphore_signal(
                barrier, inc=1, device_id={"hist": z + distance}, device_id_type=MESH
            )

    for t, h, other_rank in peer_ranks:

        @pl.when(other_rank > rank)
        def _(t=t, h=h):
            pl.semaphore_signal(barrier, inc=1, device_id=tower_id(t, h), device_id_type=MESH)

    mine_cols = pl.ds(pl.multiple_of(c * hidden, 128), hidden)
    mate_cols = pl.ds(pl.multiple_of(mate * hidden, 128), hidden)
    q_loads = [
        pltpu.make_async_copy(q_hbm.at[:, i * width : (i + 1) * width], q_all.at[z, i], q_load)
        for i in range(chunks)
    ]
    loads = [
        pltpu.make_async_copy(src, dst, load_sem.at[i])
        for i, (src, dst) in enumerate(
            [
                (user_hbm, u_all.at[z]),
                (bucket_hbm, bucket),
                (tbias_hbm, tbias),
                (len_hbm, len_ref),
                (k_hbm, k_buf),
                (v_hbm, v_buf),
                (gate_hbm, gate.at[2 * x + c]),
                (b_hbm.at[:, mine_cols], b_buf),
                (o_hbm.at[:, mine_cols], o_buf),
                (w_hbm.at[:, mine_cols], w_buf.at[c]),
            ]
        )
    ]
    user_load, bucket_load, tbias_load, len_load, k_load, v_load, *late_loads = loads
    for load in q_loads + loads[:6]:
        load.start()

    awaited = rank + z

    @pl.when(awaited > 0)
    def _():
        pl.semaphore_wait(barrier, awaited)

    for distance in range(1, n_hist):

        @pl.when(z >= distance)
        def _(distance=distance):
            pl.semaphore_signal(
                above.at[z - 1], inc=1, device_id={"hist": z - distance}, device_id_type=MESH
            )

    for t, h, other_rank in peer_ranks:

        @pl.when(other_rank < rank)
        def _(t=t, h=h):
            pl.semaphore_signal(peers, inc=1, device_id=tower_id(t, h), device_id_type=MESH)

    def remote(src, dst, send, recv, device_id):
        return pltpu.make_async_remote_copy(
            src_ref=src,
            dst_ref=dst,
            send_sem=send,
            recv_sem=recv,
            device_id=device_id,
            device_id_type=MESH,
        )

    def slot_of(block, at):
        return lax.rem(block - at + n_hist, n_hist) - 1

    def query_copy(there, chunk):
        return remote(
            q_all.at[z, chunk],
            q_all.at[z, chunk],
            q_send,
            q_recv.at[slot_of(z, there), chunk],
            {"hist": there},
        )

    def user_copy(there):
        return remote(u_all.at[z], u_all.at[z], u_send, u_recv.at[slot_of(z, there)], {"hist": there})

    def send_queries(there):
        user_copy(there).start()
        for chunk in range(chunks):
            query_copy(there, chunk).start()

    places = [(at, core) for at in range(n_hist) for core in range(2)]
    place = 2 * z + c

    def flag(values):
        chosen = pick(place, [int(v) for v in values])
        return bool(chosen) if isinstance(chosen, int) else chosen == 1

    def goes_direct(distance, sign):
        return flag(
            [
                not relayed(at, at + sign * distance, n_hist, core)
                if 0 <= at + sign * distance < n_hist
                else False
                for at, core in places
            ]
        )

    def send_down(distance):
        @pl.when(z >= distance)
        def _():
            when(goes_direct(distance, -1))(lambda: send_queries(z - distance))

    def send_up(distance, condition):
        @pl.when(condition)
        def _():
            pl.semaphore_wait(above.at[z + distance - 1], 1)
            when(goes_direct(distance, 1))(lambda: send_queries(z + distance))

    user_load.wait()
    pltpu.make_async_copy(q_all.at[z], q_all.at[z], q_load).wait()
    for distance in range(n_hist - 1, 0, -1):
        send_down(distance)

    send_up(1, z < n_hist - 2)

    bucket_load.wait()
    tbias_load.wait()
    len_load.wait()
    heads, bucket_count = tbias.shape
    half_scale = 0.5 * DH ** (-0.5)
    tb = tbias[...] * 0.5
    bias_rows, owner_rows = [], []
    for u in range(users):
        onehot = jnp.where(
            lax.broadcasted_iota(jnp.int32, (bucket_count, per_user), 0) == bucket[u : u + 1, :],
            1.0,
            0.0,
        ).astype(F32)
        bias_rows.append(
            lax.dot_general(
                tb,
                onehot,
                (((1,), (0,)), ((), ())),
                precision=lax.Precision.HIGHEST,
                preferred_element_type=F32,
            )
        )
        position = z * per_user + lax.broadcasted_iota(jnp.int32, (1, per_user), 1)
        owner_rows.append(jnp.where(position < len_ref[:, u : u + 1], u, -1))
    bias = jnp.concatenate(bias_rows, axis=1)
    owner = jnp.concatenate(owner_rows, axis=1)
    events = users * per_user
    k_load.wait()
    v_load.wait()

    def live_of(index):
        user_col = jnp.broadcast_to(u_all[index], (128, rows)).T[:, :1]
        return jnp.where(user_col == owner, 1.0, 0.0).astype(F32)

    def scored(query, head):
        cols = slice(head * DH, (head + 1) * DH)
        return lax.dot_general(
            query,
            k_buf[:, :, cols].reshape(events, DH),
            (((1,), (1,)), ((), ())),
            preferred_element_type=F32,
        )

    def weighed(s, live, head):
        half = s * half_scale + bias[head : head + 1, :]
        return ((half + half * jnp.tanh(half)) * live).astype(BF16)

    def gathered(weight, head):
        cols = slice(head * DH, (head + 1) * DH)
        return jnp.dot(
            weight, v_buf[:, :, cols].reshape(events, DH), preferred_element_type=F32
        )

    per_chunk = heads // chunks

    def share_of(block, live, chunk):
        mine = [chunk * per_chunk + i for i in range(per_chunk)]
        s = [scored(q_all[block, chunk, :, i * DH : (i + 1) * DH], head) for i, head in enumerate(mine)]
        weights = [weighed(s[i], live, head) for i, head in enumerate(mine)]
        parts = [gathered(weights[i], head) for i, head in enumerate(mine)]
        return jnp.concatenate(parts, axis=1) if per_chunk > 1 else parts[0]

    own_live = live_of(z)
    for chunk in range(chunks):
        own_share[chunk] = share_of(z, own_live, chunk)

    for load in late_loads:
        load.start()

    send_up(1, z == n_hist - 2)
    for distance in range(2, n_hist):
        send_up(distance, z + distance < n_hist)


    @pl.when(rank < 2 * n_tower - 1)
    def _():
        pl.semaphore_wait(peers, 2 * n_tower - 1 - rank)
    w_copy = remote(
        w_hbm.at[:, mate_cols], w_buf.at[c], w_send.at[0], w_recv.at[0], {"head": mate}
    )
    w_copy.start()
    for i, (t, h) in enumerate(tower_peers):
        copy = remote(
            gate_hbm, gate.at[2 * x + c], gate_send, gate_recv.at[2 * x + c], tower_id(t, h)
        )
        copy.start()

    def user_arrives(block):
        remote(
            u_all.at[block], u_all.at[block], u_send, u_recv.at[slot_of(block, z)], {"hist": block}
        ).wait_recv()

    def query_arrives(block, chunk):
        remote(
            q_all.at[block, chunk],
            q_all.at[block, chunk],
            q_send,
            q_recv.at[slot_of(block, z), chunk],
            {"hist": block},
        ).wait_recv()

    def pass_copy(step, block, there, chunk):
        return remote(
            q_all.at[block, chunk],
            q_all.at[block, chunk],
            q_send,
            q_recv.at[slot_of(block, there), chunk],
            {"hist": there},
        )

    def pass_user(step, block, there):
        return remote(
            u_all.at[block],
            u_all.at[block],
            u_send,
            u_recv.at[slot_of(block, there)],
            {"hist": there},
        )

    def share_copy(step, chunk):
        return remote(
            share_out.at[step, chunk],
            share_in.at[z, chunk],
            share_send,
            share_recv.at[slot_of(z, steps[step][0]), chunk],
            {"hist": steps[step][0]},
        )

    orders = [order_of(at, n_hist, core) for at, core in places]
    steps = []
    for step in range(n_hist - 1):
        blocks = [order[step] for order in orders]
        targets = [handed_on(b, at, n_hist, core) for b, (at, core) in zip(blocks, places)]
        steps.append(
            (
                pick(place, blocks),
                flag([there is not None for there in targets]),
                pick(place, [there or 0 for there in targets]),
            )
        )

    for step, (block, passing, there) in enumerate(steps):
        user_arrives(block)

        @when(passing)
        def _():
            pass_user(step, block, there).start()

        live = live_of(block)
        holding = not passing if isinstance(passing, bool) else jnp.logical_not(passing)

        @when(passing)
        def _():
            for chunk in range(chunks):
                query_arrives(block, chunk)
                pass_copy(step, block, there, chunk).start()

        for chunk in range(chunks):
            @when(holding)
            def _():
                query_arrives(block, chunk)

            share_out[step, chunk] = share_of(block, live, chunk).astype(BF16)
            share_copy(step, chunk).start()

    sources = [block for block, _, _ in steps]

    def att_copy(tower, head, chunk, device_id):
        return remote(
            att_buf.at[2 * tower + head, chunk],
            att_buf.at[2 * tower + head, chunk],
            att_send,
            att_recv.at[2 * tower + head],
            device_id,
        )

    own = []
    for chunk in range(chunks):
        for src in sources:
            remote(
                share_out.at[0, chunk],
                share_in.at[src, chunk],
                share_send,
                share_recv.at[slot_of(src, z), chunk],
                {"hist": src},
            ).wait_recv()
        part = own_share[chunk]
        for src in sources:
            part = part + share_in[src, chunk].astype(F32)
        own.append(part)
        att_buf[2 * x + c, chunk] = part.astype(BF16)
        for t in range(1, n_tower):
            for head in range(2):
                att_copy(x, c, chunk, {"tower": partner_of(x, t, n_tower), "head": head}).start()
        att_copy(x, c, chunk, {"head": mate}).start()

    def half_arrives(tower, head):
        remote(
            gate_hbm, gate.at[2 * tower + head], gate_send, gate_recv.at[2 * tower + head], {"head": mate}
        ).wait_recv()
        remote(
            att_buf.at[2 * tower + head],
            att_buf.at[2 * tower + head],
            att_send,
            att_recv.at[2 * tower + head],
            {"head": mate},
        ).wait_recv()

    def half_of(tower, head):
        return [att_buf[2 * tower + head, chunk].astype(F32) for chunk in range(chunks)]

    def normalised(pieces, gates):
        every = [p for half in pieces for p in half]
        row_sum = sum(jnp.sum(p, axis=1, keepdims=True) for p in every)
        row_squares = sum(jnp.sum(p * p, axis=1, keepdims=True) for p in every)
        row_mean = row_sum / total_feat
        row_var = row_squares / total_feat - row_mean * row_mean
        scale = lax.rsqrt(row_var + 1e-05)
        return [
            ((jnp.concatenate(half, axis=1) - row_mean) * scale * g.astype(F32)).astype(BF16)
            for half, g in zip(pieces, gates)
        ]

    for load in late_loads:
        load.wait()
    remote(
        w_hbm.at[:, mate_cols], w_buf.at[mate], w_send.at[0], w_recv.at[0], {"head": mate}
    ).wait_recv()

    def scores_of(first, first_w, second, second_w):
        pre = jnp.dot(first, w_buf[first_w], preferred_element_type=F32)
        pre = pre + jnp.dot(second, w_buf[second_w], preferred_element_type=F32)
        half = (pre + b_buf[...]) * 0.5
        part = (half + half * jnp.tanh(half)) * o_buf[...]
        acc = part[:, 0:128]
        for i in range(1, hidden // 128):
            acc = acc + part[:, i * 128 : (i + 1) * 128]
        return jnp.sum(acc.T, axis=0, keepdims=True)

    half_arrives(x, mate)
    mine, theirs = normalised([own, half_of(x, mate)], [gate[2 * x + c], gate[2 * x + mate]])
    states_out[...] = mine
    own_scores = scores_of(mine, c, theirs, mate)
    score_in[2 * x + c] = own_scores
    copy = remote(
        score_in.at[2 * x + c], score_in.at[2 * x + c], score_send_sem, score_recv.at[2 * x + c], {"head": mate}
    )
    copy.start()
    for t in range(1, n_tower):
        other = source_of(x, t, n_tower)
        half_arrives(other, c)
        half_arrives(other, mate)
        first, second = normalised(
            [half_of(other, 0), half_of(other, 1)], [gate[2 * other], gate[2 * other + 1]]
        )
        score_send[t] = scores_of(first, 0, second, 1)
        for h in range(2):
            copy = remote(
                score_send.at[t],
                score_in.at[2 * x + c],
                score_send_sem,
                score_recv.at[2 * x + c],
                {"tower": other, "head": h},
            )
            copy.start()

    for t, h in tower_peers:
        tower, head = partner_of(x, t, n_tower), mate if h else c
        remote(
            score_in.at[2 * tower + head],
            score_in.at[2 * tower + head],
            score_send_sem,
            score_recv.at[2 * tower + head],
            {"head": mate},
        ).wait_recv()
    total = score_in[0] + score_in[1]
    for t in range(1, n_tower):
        total = total + (score_in[2 * t] + score_in[2 * t + 1])
    scores_out[...] = total
    w_copy.wait_send()
    sent = [
        sum(
            (not relayed(at, b, n_hist, core)) + (handed_on(b, at, n_hist, core) is not None)
            for b in range(n_hist)
            if b != at
        )
        for at, core in places
    ]
    for count in sorted(set(sent)):

        @when(flag([n == count for n in sent]))
        def _(count=count):
            for ref, send, recv in (
                (q_all.at[0:count], q_send, q_recv.at[0, 0]),
                (u_all.at[0:count], u_send, u_recv.at[0]),
            ):
                remote(ref, ref, send, recv, {"head": mate}).wait_send()

    others, peer_count = slice(0, n_hist - 1), slice(0, 2 * n_tower - 1)
    for ref, send, recv in (
        (share_out.at[others], share_send, share_recv.at[0, 0]),
        (gate.at[peer_count], gate_send, gate_recv.at[0]),
        (att_buf.at[peer_count], att_send, att_recv.at[0]),
        (score_in.at[peer_count], score_send_sem, score_recv.at[0]),
    ):
        remote(ref, ref, send, recv, {"head": mate}).wait_send()


def hand_over(states_in, scores_in, states_out, scores_out, sems):
    copies = [
        pltpu.make_async_copy(states_in, states_out, sems.at[0]),
        pltpu.make_async_copy(scores_in, scores_out, sems.at[1]),
    ]
    for copy in copies:
        copy.start()
    for copy in copies:
        copy.wait()


def local(
    queries,
    hist_keys,
    hist_values,
    cand_user,
    time_bucket,
    hist_len,
    cand_gate,
    time_bias,
    tower_in,
    tower_bias,
    tower_out,
    *,
    n_hist,
    n_tower,
):
    rows, feat = queries.shape
    hidden = tower_in.shape[1] // 2
    chunks = CHUNKS if (feat // DH) % CHUNKS == 0 else 1
    width = feat // chunks
    any_spec = pl.BlockSpec(memory_space=pl.ANY)
    vmem_spec = pl.BlockSpec(memory_space=pltpu.VMEM)
    dma = pltpu.SemaphoreType.DMA
    states, scores = pl.pallas_call(
        functools.partial(kernel, n_hist, n_tower),
        out_shape=(
            pltpu.VMEM((rows, feat), BF16),
            pltpu.VMEM((1, rows), F32),
        ),
        in_specs=[any_spec] * 11,
        out_specs=(vmem_spec, vmem_spec),
        scratch_shapes=[
            pltpu.VMEM((n_hist, chunks, rows, width), BF16),
            pltpu.VMEM((n_hist, 1, rows), jnp.int32),
            pltpu.VMEM(hist_keys.shape, BF16),
            pltpu.VMEM(hist_values.shape, BF16),
            pltpu.VMEM(time_bucket.shape, jnp.int32),
            pltpu.VMEM((1,) + hist_len.shape, jnp.int32),
            pltpu.VMEM((2 * n_tower, rows, feat), BF16),
            pltpu.VMEM(time_bias.shape[::-1], F32),
            pltpu.VMEM((2, feat, hidden), BF16),
            pltpu.VMEM((1, hidden), F32),
            pltpu.VMEM((1, hidden), F32),
            pltpu.VMEM((chunks, rows, width), F32),
            pltpu.VMEM((n_hist, chunks, rows, width), BF16),
            pltpu.VMEM((n_hist, chunks, rows, width), BF16),
            pltpu.VMEM((2 * n_tower, chunks, rows, width), BF16),
            pltpu.VMEM((n_tower, 1, rows), F32),
            pltpu.VMEM((2 * n_tower, 1, rows), F32),
            dma((10,)),
            dma,
            pltpu.SemaphoreType.REGULAR((n_hist - 1,)),
            pltpu.SemaphoreType.REGULAR,
            dma,
            dma((n_hist - 1, chunks)),
            dma,
            dma((n_hist - 1,)),
            dma,
            dma((n_hist - 1, chunks)),
            dma((1,)),
            dma((1,)),
            dma,
            dma((2 * n_tower,)),
            dma,
            dma((2 * n_tower,)),
            dma,
            dma((2 * n_tower,)),
        ],
        compiler_params=pltpu.CompilerParams(collective_id=0, has_side_effects=True),
    )(
        queries,
        hist_keys,
        hist_values,
        cand_user.reshape(1, rows),
        time_bucket,
        hist_len.reshape(1, -1),
        cand_gate,
        time_bias.T,
        tower_in,
        tower_bias.reshape(1, -1),
        tower_out.reshape(1, -1),
    )
    states, scores = pl.pallas_call(
        hand_over,
        out_shape=(
            jax.ShapeDtypeStruct((rows, feat), BF16),
            jax.ShapeDtypeStruct((1, rows), F32),
        ),
        in_specs=[vmem_spec, vmem_spec],
        out_specs=(any_spec, any_spec),
        scratch_shapes=[dma((2,))],
    )(
        pltpu.with_memory_space_constraint(states, pltpu.VMEM),
        pltpu.with_memory_space_constraint(scores, pltpu.VMEM),
    )
    return states, scores.reshape(rows)


def solution(mesh):
    return jax.shard_map(
        functools.partial(local, n_hist=mesh.shape["hist"], n_tower=mesh.shape["tower"]),
        mesh=mesh,
        in_specs=(
            P(("groups", "hist", "tower"), "head"),
            P("groups", "hist", "head"),
            P("groups", "hist", "head"),
            P(("groups", "hist", "tower")),
            P("groups", "hist"),
            P("groups"),
            P(("groups", "hist", "tower"), "head"),
            P(None, "head"),
            P("head", "tower"),
            P("tower"),
            P("tower"),
        ),
        out_specs=(P(("groups", "hist", "tower"), "head"), P(("groups", "hist", "tower"))),
        check_vma=False,
    )
```
